256 devices in a mesh: ctx: 64 (over z, y, core), tp: 4 (over x).
Axes of the slice: x: 4, y: 4, z: 8, core: 2. Of those that a mesh axis runs over, the one named last changes fastest.
Arguments:
- projected: bfloat16 [8192, 4, 4640], P('ctx', 'tp'), may hold values from -6 to 6
- conv_weight: float32 [4, 4, 2560], P('tp'), may hold values from -3 to 3
- conv_bias: float32 [4, 2560], P('tp'), may hold values from -1.5 to 1.5
- step_bias: float32 [4, 32], P('tp'), may hold values from -1 to 0.5
- log_rates: float32 [4, 32], P('tp'), as said below
- norm_gain: float32 [4, 2048], P('tp'), may hold values from 0.1 to 1.9
- out_weight: bfloat16 [4, 2048, 4096], P('tp', 'ctx'), may hold values from -0.0625 to 0.0625
Outputs:
- mixed: bfloat16 [8192, 4096], P('ctx', 'tp')
The draws below stay inside these ranges and needn't reach their ends.
Inputs may be any that keep to these rules, and one draw needn't show every extreme that they name: log_rates lies between log(0.3 / 8192) and log(1 / 25).
All inputs are finite; a program needn't handle non-finite values.
Results may differ from the reference program's by a relative error of at most 0.0058.
Values may be sent and summed in bfloat16 or wider, within the bound.
No kernel may reach another device: no remote copies, remote signals or barrier semaphores. Data moves between devices by JAX's collectives and lax.ppermute only.
A program may use at most 320 MiB of HBM per device.

```python
import math
import jax
import jax.numpy as jnp
from jax import lax

D = 4096
GROUPS = 4
HPG = 32
P_SIZE = 64
N = 256
KCONV = 4
SPAN = 128
TOKENS = 8192
GCH = 2048
GCONV = 2560
GCOLS = 4640


def draw_log_rates(key, part):
    slow_key, slow_rate_key, fast_key = jax.random.split(jax.random.fold_in(key, 7), 3)
    array_shape = (GROUPS, HPG)
    slow_share = 0.5
    slow_heads = jax.random.bernoulli(slow_key, slow_share, array_shape)
    slow_rates = jnp.exp(jax.random.uniform(slow_rate_key, array_shape, jnp.float32, math.log(0.3), math.log(2.0))) / TOKENS
    fast_rates = jnp.exp(jax.random.uniform(fast_key, array_shape, jnp.float32, math.log(1.0 / 50.0), math.log(1.0 / 25.0)))
    return jnp.log(jnp.where(slow_heads, slow_rates, fast_rates)).astype(jnp.float32)


def shard_levels(rng, extent, cuts, low, largest):
    def one(position, shards_of):
        draws = jax.random.uniform(jax.random.fold_in(jax.random.fold_in(rng, 6), position), (shards_of,), jnp.float32, low / len(cuts), largest / len(cuts))
        return jnp.repeat(jnp.exp(draws), extent[position] // shards_of).reshape((-1,) + (1,) * (len(extent) - position - 1))

    level = one(*cuts[0])
    for cut in cuts[1:]:
        level = level * one(*cut)
    return level


def normal_values(key, shape, scale, most, shards=(), kind=jnp.bfloat16):
    values = jax.random.normal(key, shape, jnp.float32) * scale
    if len(shards) > 0:
        values = shard_levels(key, shape, shards, -0.22, 0.18) * values
    return jnp.clip(values, min=-most, max=most).astype(kind)


def setup_inputs(seed: int = 0) -> dict:
    splits = jax.random.split(jax.random.key(seed), 8)
    return {
        "projected": normal_values(splits[0], (TOKENS, GROUPS, GCOLS), 1.0, 6.0, ((0, 64), (1, 4))),
        "conv_weight": normal_values(splits[1], (GROUPS, KCONV, GCONV), KCONV ** -0.5, 3.0, ((0, 4),), jnp.float32),
        "conv_bias": normal_values(splits[2], (GROUPS, GCONV), 0.3, 1.5, ((0, 4),), jnp.float32),
        "step_bias": jnp.clip(-1.0 + 1.5 * jax.random.uniform(splits[3], (GROUPS, HPG), jnp.float32) ** shard_levels(splits[3], (GROUPS, HPG), ((0, 4),), -0.2, 0.2), -1.0, 0.5),
        "log_rates": draw_log_rates(jax.random.fold_in(splits[7], 71), 0),
        "norm_gain": jnp.clip(1.0 + 0.18 * jax.random.normal(splits[5], (GROUPS, GCH), jnp.float32), 0.1, 1.9),
        "out_weight": normal_values(splits[6], (GROUPS, GCH, D), (GROUPS * GCH) ** -0.5, 0.0625, ((0, 4), (1, 64))),
    }


highest_precision = lax.Precision.HIGHEST

def ssd_blocks(inputs_x, step_sizes, decay_rate, b_rows, c_rows, block_rows):
    row_count = inputs_x.shape[0]
    block_count = row_count // block_rows
    head_count = inputs_x.shape[1]
    head_width = inputs_x.shape[2]
    state_count = b_rows.shape[1]
    x_blocks = inputs_x.reshape(block_count, block_rows, head_count, head_width)
    step_blocks = step_sizes.reshape(block_count, block_rows, head_count)
    b_blocks = b_rows.reshape(block_count, block_rows, state_count)
    c_blocks = c_rows.reshape(block_count, block_rows, state_count)
    causal_mask = (jnp.arange(block_rows)[:, None] >= jnp.arange(block_rows)[None, :])[None]

    def advance(carried, pieces):
        x_block, step_block, b_block, c_block = pieces
        log_steps = step_block * decay_rate[None, :]
        running = jnp.cumsum(log_steps, axis=0)
        intersection = jnp.dot(c_block, b_block.T, precision=highest_precision)
        log_gaps = running.T[:, :, None] - running.T[:, None, :]
        factors = jnp.where(causal_mask, jnp.exp(jnp.where(causal_mask, log_gaps, 0.0)), 0.0)
        factors = factors * intersection[None] * step_block.T[:, None, :]
        within = jnp.einsum('hts,shp->thp', factors, x_block, precision=highest_precision)
        carried_part = jnp.einsum('tn,hpn->thp', c_block, carried, precision=highest_precision) * jnp.exp(running)[:, :, None]
        tail_weight = jnp.exp(running[-1][None, :] - running) * step_block
        weighted = x_block * tail_weight[:, :, None]
        updated = carried * jnp.exp(running[-1])[:, None, None] + jnp.einsum('shp,sn->hpn', weighted, b_block, precision=highest_precision)
        return (updated, within + carried_part)
    initial = jnp.zeros((head_count, head_width, state_count), jnp.float32)
    final_state, outputs = lax.scan(advance, initial, (x_blocks, step_blocks, b_blocks, c_blocks))
    total_log = lax.optimization_barrier(jnp.sum(step_sizes * decay_rate[None, :], axis=0))
    return (outputs.reshape(row_count, head_count, head_width), final_state, total_log)

def reference(projected, conv_weight, conv_bias, step_bias, log_rates, norm_gain, out_weight):
    row_count = projected.shape[0]
    summed = jnp.zeros((row_count, D), jnp.float32)
    for group in range(GROUPS):
        conv_input = projected[:, group, GCH:GCH + GCONV].astype(jnp.float32)
        padded = jnp.concatenate([jnp.zeros((KCONV - 1, GCONV), jnp.float32), conv_input], axis=0)
        mixed_conv = conv_bias[group][None, :]
        for offset in range(KCONV):
            mixed_conv = mixed_conv + conv_weight[group, offset][None, :] * padded[offset:offset + row_count]
        activated = jax.nn.silu(mixed_conv).astype(jnp.bfloat16)
        step_sizes = jax.nn.softplus(projected[:, group, GCH + GCONV:].astype(jnp.float32) + step_bias[group][None, :])
        decay_rate = -jnp.exp(log_rates[group])
        values = activated[:, :GCH].astype(jnp.float32).reshape(row_count, HPG, P_SIZE)
        b_rows = activated[:, GCH:GCH + N].astype(jnp.float32)
        c_rows = activated[:, GCH + N:].astype(jnp.float32)
        outputs, final_state, total_log = ssd_blocks(values, step_sizes, decay_rate, b_rows, c_rows, SPAN)
        scanned = outputs.reshape(row_count, GCH).astype(jnp.bfloat16)
        gated = scanned.astype(jnp.float32) * jax.nn.silu(projected[:, group, :GCH].astype(jnp.float32))
        normed = (gated * lax.rsqrt(lax.optimization_barrier(jnp.mean(gated * gated, axis=1, keepdims=True)) + 1e-05) * norm_gain[group][None, :]).astype(jnp.bfloat16)
        summed = summed + jnp.dot(normed, out_weight[group], preferred_element_type=jnp.float32)
    return summed.astype(jnp.bfloat16)
```

```python
import jax
import jax.numpy as jnp
from jax import lax
from jax.experimental import pallas as pl
from jax.experimental.pallas import tpu as pltpu
from jax.sharding import Mesh
from jax.sharding import PartitionSpec as P

P_SIZE = 64
N = 256
KCONV = 4
ROWS = 128
PAIR = 256
GCH = 2048
GCONV = 2560
GCOLS = 4640
HALF = 1024
HEADS = 16
BLOCK = 512
Z, Y, C, T = 8, 4, 2, 4
CHIPS = Z * Y
f32, bf16 = jnp.float32, jnp.bfloat16
MIB = 1 << 20


def params(mib):
    return pltpu.CompilerParams(vmem_limit_bytes=mib * MIB)


def vmem():
    return pl.BlockSpec(memory_space=pltpu.VMEM)


def smem():
    return pl.BlockSpec(memory_space=pltpu.SMEM)


def dot(a, b, ca=1, cb=0, precision=None):
    return lax.dot_general(
        a, b, (((ca,), (cb,)), ((), ())), precision=precision, preferred_element_type=f32
    )


def lanes(shape):
    return lax.broadcasted_iota(jnp.int32, shape, 1)


def split_three(v):
    v = jnp.where(lanes(v.shape) < HEADS, v, 0.0)
    high = v.astype(bf16).astype(f32)
    rest = v - high
    middle = rest.astype(bf16).astype(f32)
    low = (rest - middle).astype(bf16).astype(f32)
    packed = high + pltpu.roll(middle, HEADS, 1) + pltpu.roll(low, 2 * HEADS, 1)
    return packed.astype(bf16)


def head_table(first, width):
    row = lax.broadcasted_iota(jnp.int32, (128, width), 0)
    column = lax.broadcasted_iota(jnp.int32, (128, width), 1) + first
    hit = (row < 3 * HEADS) & ((row % HEADS) == column // P_SIZE)
    return jnp.where(hit, 1.0, 0.0).astype(bf16)


def scan_kernel(
    at, mine, other, rim, taps, bias, step_bias, log_rates,
    within, keys, growth, send,
    padded, tap_rows, values, queries, raw, small,
):
    core = at[0]
    x_at = pl.multiple_of(core * HALF, 128)
    mine_at = pl.multiple_of(core * ROWS, 128)
    other_at = pl.multiple_of((1 - core) * ROWS, 128)
    padded[0:8, 0:HALF] = rim[:, pl.ds(x_at, HALF)].astype(f32)
    padded[0:8, HALF:] = rim[:, GCH:GCONV].astype(f32)
    z_end = pl.multiple_of(GCH + x_at, 128)
    for rows, ref in ((mine_at, mine), (other_at, other)):
        target = pl.ds(pl.multiple_of(8 + rows, 8), ROWS)
        padded[target, 0:HALF] = ref[:, pl.ds(z_end, HALF)].astype(f32)
        padded[target, HALF:] = ref[:, 2 * GCH : GCH + GCONV].astype(f32)
        raw[pl.ds(rows, ROWS), :] = jnp.zeros((ROWS, 128), f32)
        raw[pl.ds(rows, ROWS), 0:32] = ref[:, GCH + GCONV : GCOLS].astype(f32)
    tap_rows[0:KCONV, 0:HALF] = taps[:, pl.ds(x_at, HALF)]
    tap_rows[0:KCONV, HALF:] = taps[:, GCH:GCONV]
    tap_rows[4:5, 0:HALF] = bias[:, pl.ds(x_at, HALF)]
    tap_rows[4:5, HALF:] = bias[:, GCH:GCONV]
    small[...] = jnp.zeros((8, 128), f32)
    small[0:1, 0:32] = step_bias[...]
    small[1:2, 0:32] = log_rates[...]

    for c0 in range(0, HALF + 2 * N, 256):
        for r0 in range(0, PAIR, 64):
            total = jnp.broadcast_to(tap_rows[4:5, c0 : c0 + 256], (64, 256))
            for k in range(KCONV):
                total = total + tap_rows[k : k + 1, c0 : c0 + 256] * padded[
                    5 + k + r0 : 5 + k + r0 + 64, c0 : c0 + 256
                ]
            active = (total * jax.nn.sigmoid(total)).astype(bf16)
            if c0 < HALF:
                values[r0 : r0 + 64, c0 : c0 + 256] = active
            elif c0 == HALF:
                keys[r0 : r0 + 64, :] = active
            else:
                queries[r0 : r0 + 64, :] = active

    first = core == 0

    def own(v):
        return jnp.where(first, v, pltpu.roll(v, 128 - HEADS, 1))

    head_lane = lanes((PAIR, 128)) < HEADS
    steps = own(raw[...] + small[0:1, :])
    steps = jnp.where(head_lane, jax.nn.softplus(steps), 0.0)
    rate = -jnp.exp(own(jnp.broadcast_to(small[1:2, :], (8, 128))))[0:1]
    logs = steps * rate
    row = lax.broadcasted_iota(jnp.int32, (PAIR, PAIR), 0)
    column = lax.broadcasted_iota(jnp.int32, (PAIR, PAIR), 1)
    running = dot(jnp.where(row >= column, 1.0, 0.0), logs, precision=lax.Precision.HIGHEST)
    running_t = running.T
    steps_t = steps.T
    growth[...] = split_three(jnp.exp(running))

    causal = row[:ROWS, :ROWS] >= column[:ROWS, :ROWS]
    products = []
    for a in (0, ROWS):
        own_product = dot(queries[a : a + ROWS, :], keys[a : a + ROWS, :], 1, 1)
        products.append(jnp.where(causal, own_product, 0.0))
    across = dot(queries[ROWS:, :], keys[:ROWS, :], 1, 1).astype(bf16)
    low_lane = lanes((ROWS, 128)) < P_SIZE
    for pair in range(HEADS // 2):
        c0 = pair * 128
        for i, a in enumerate((0, ROWS)):
            x = values[a : a + ROWS, c0 : c0 + 128]
            parts = []
            for h in (2 * pair, 2 * pair + 1):
                gap = running[a : a + ROWS, h : h + 1] - running_t[h : h + 1, a : a + ROWS]
                factor = products[i] * jnp.exp(jnp.minimum(gap, 0.0)) * steps_t[h : h + 1, a : a + ROWS]
                parts.append(dot(factor.astype(bf16), x))
            within[a : a + ROWS, c0 : c0 + 128] = jnp.where(low_lane, parts[0], parts[1])

    middle = running[ROWS - 1 : ROWS, :]
    end = running[PAIR - 1 : PAIR, :]
    to_end = split_three(jnp.exp(end - running) * steps)
    to_middle = split_three(jnp.exp(middle - running[:ROWS]) * steps[:ROWS])
    from_middle = split_three(jnp.exp(running[ROWS:] - middle))
    all_logs = split_three(jnp.broadcast_to(end, (PAIR, 128)))
    keys_t = keys[...].astype(f32).T.astype(bf16)
    for c0 in range(0, HALF, 256):
        table = head_table(c0, 256)
        x = values[:, c0 : c0 + 256].astype(f32)
        entering = dot(across, (x[:ROWS] * dot(to_middle, table)).astype(bf16))
        within[ROWS:, c0 : c0 + 256] += entering * dot(from_middle, table)
        weighted = (x * dot(to_end, table)).astype(bf16)
        send[:, c0 : c0 + 256] = dot(keys_t, weighted).astype(bf16)
    send[:, HALF:] = all_logs
    keys[...] = queries[...]


def prefix_kernel(got, back, decays):
    for c0 in range(0, HALF, 256):
        decays[:, c0 : c0 + 256] = jnp.exp(dot(got[:, HALF:], head_table(c0, 256)))
    state = jnp.zeros((8, HALF), f32)
    for pair in range(CHIPS // 2):
        rows = slice(16 * pair, 16 * pair + 16)
        local = got[rows, 0:HALF].astype(f32)
        decay = decays[rows, :]
        second = state * decay[:8] + local[:8]
        back[rows, :] = jnp.concatenate([state, second], axis=0).astype(bf16)
        state = second * decay[8:] + local[8:]


def carried_kernel(within, queries, growth, state, scanned):
    for c0 in range(0, HALF, 256):
        carried = dot(queries[...], state[:, c0 : c0 + 256])
        carried = carried * dot(growth[...], head_table(c0, 256))
        scanned[:, c0 : c0 + 256] = (within[:, c0 : c0 + 256] + carried).astype(bf16)


def norm_kernel(at, scanned, scanned_other, gate, gate_other, gain, normed, whole, gates):
    core = at[0]
    own_at = pl.multiple_of(core * HALF, 128)
    other_at = pl.multiple_of((1 - core) * HALF, 128)
    whole[:, pl.ds(own_at, HALF)] = scanned[...]
    whole[:, pl.ds(other_at, HALF)] = scanned_other[...]
    gates[pl.ds(pl.multiple_of(core * ROWS, 128), ROWS), :] = gate[...]
    gates[pl.ds(pl.multiple_of((1 - core) * ROWS, 128), ROWS), :] = gate_other[...]

    def body(i, carry):
        rows = pl.ds(pl.multiple_of(i * 16, 16), 16)
        g = gates[rows, :].astype(f32)
        gated = whole[rows, :].astype(f32) * (g * jax.nn.sigmoid(g))
        scale = lax.rsqrt(jnp.mean(gated * gated, axis=1, keepdims=True) + 1e-05)
        normed[rows, :] = (gated * scale * gain[...]).astype(bf16)
        return carry

    lax.fori_loop(0, PAIR // 16, body, 0)


def project_kernel(at, normed, weight, out, total):
    step = pl.program_id(0)

    @pl.when(step == 0)
    def _():
        total[...] = jnp.zeros_like(total)

    total[...] += dot(normed[...], weight[...])

    @pl.when(step == pl.num_programs(0) - 1)
    def _():
        out[...] = total[...].astype(out.dtype)


def project(block, normed, weight, dtype):
    depth = 512
    return pl.pallas_call(
        project_kernel,
        out_shape=jax.ShapeDtypeStruct((PAIR, BLOCK), dtype),
        grid_spec=pltpu.PrefetchScalarGridSpec(
            num_scalar_prefetch=1,
            grid=(GCH // depth,),
            in_specs=[
                pl.BlockSpec((PAIR, depth), lambda k, at: (0, k)),
                pl.BlockSpec((depth, BLOCK), lambda k, at: (k, at[0])),
            ],
            out_specs=pl.BlockSpec((PAIR, BLOCK), lambda k, at: (0, 0)),
            scratch_shapes=[pltpu.VMEM((PAIR, BLOCK), f32)],
        ),
        cost_estimate=pl.CostEstimate(
            flops=2 * PAIR * GCH * BLOCK, bytes_accessed=2 * GCH * BLOCK, transcendentals=0
        ),
        compiler_params=params(24),
        name="project",
    )(block, normed, weight)


def add_kernel(at, own, a, b, c, keep, away):
    core = at[0]
    for ref, which in ((keep, core), (away, 1 - core)):
        rows = pl.ds(pl.multiple_of(which * ROWS, 128), ROWS)
        total = own[rows, :] + a[rows, :].astype(f32) + b[rows, :].astype(f32)
        ref[...] = (total + c[rows, :].astype(f32)).astype(bf16)


def join_kernel(at, keep, got, out):
    core = at[0]
    out[:, pl.ds(pl.multiple_of(core * BLOCK, 128), BLOCK)] = keep[...]
    out[:, pl.ds(pl.multiple_of((1 - core) * BLOCK, 128), BLOCK)] = got[...]


def shape(*dims, dtype=bf16):
    return jax.ShapeDtypeStruct(dims, dtype)


def on_device(projected, conv_weight, conv_bias, step_bias, log_rates, norm_gain, out_weight):
    weight = lax.all_gather(out_weight[0], ("z", "y", "c"), axis=0, tiled=True)
    mine = projected.reshape(ROWS, GCOLS)
    swap = [(0, 1), (1, 0)]
    other = lax.ppermute(mine, "c", swap)
    tail = mine[ROWS - 8 :, GCH : GCH + GCONV]
    all_axes = ("z", "y", "c")
    rim_0 = lax.ppermute(tail, all_axes, [(2 * i + 1, 2 * i + 2) for i in range(CHIPS - 1)])
    rim_1 = lax.ppermute(tail, all_axes, [(2 * i + 1, 2 * i + 3) for i in range(CHIPS - 1)])
    core, tp = lax.axis_index("c"), lax.axis_index("tp")
    rim = jnp.where(core == 0, rim_0, rim_1)
    at = core.astype(jnp.int32).reshape(1)

    within, queries, growth, send = pl.pallas_call(
        scan_kernel,
        out_shape=(
            shape(PAIR, HALF, dtype=f32), shape(PAIR, N), shape(PAIR, 128), shape(N, HALF + 128),
        ),
        in_specs=[smem()] + [vmem()] * 7,
        out_specs=(vmem(),) * 4,
        scratch_shapes=[
            pltpu.VMEM((PAIR + 8, HALF + 2 * N), f32),
            pltpu.VMEM((8, HALF + 2 * N), f32),
            pltpu.VMEM((PAIR, HALF), bf16),
            pltpu.VMEM((PAIR, N), bf16),
            pltpu.VMEM((PAIR, 128), f32),
            pltpu.VMEM((8, 128), f32),
        ],
        cost_estimate=pl.CostEstimate(
            flops=1 << 29, bytes_accessed=5 * MIB, transcendentals=1 << 20
        ),
        compiler_params=params(32),
        name="scan",
    )(at, mine, other, rim, conv_weight[0], conv_bias, step_bias, log_rates)

    got = lax.all_to_all(send, ("z", "y"), 0, 0, tiled=True)
    back = pl.pallas_call(
        prefix_kernel,
        out_shape=shape(N, HALF),
        in_specs=[vmem()],
        out_specs=vmem(),
        scratch_shapes=[pltpu.VMEM((N, HALF), f32)],
        cost_estimate=pl.CostEstimate(flops=1 << 26, bytes_accessed=MIB, transcendentals=1 << 18),
        compiler_params=params(16),
        name="prefix",
    )(got)
    state = lax.all_to_all(back, ("z", "y"), 0, 0, tiled=True)
    scanned = pl.pallas_call(
        carried_kernel,
        out_shape=shape(PAIR, HALF),
        in_specs=[vmem()] * 4,
        out_specs=vmem(),
        cost_estimate=pl.CostEstimate(flops=1 << 28, bytes_accessed=2 * MIB, transcendentals=0),
        compiler_params=params(16),
        name="carried",
    )(within, queries, growth, state)
    scanned_other = lax.ppermute(scanned, "c", swap)

    gate = pl.BlockSpec((ROWS, GCH), lambda i: (0, 0))
    whole = pl.BlockSpec((PAIR, HALF), lambda i: (0, 0))
    normed = pl.pallas_call(
        norm_kernel,
        grid=(1,),
        out_shape=shape(PAIR, GCH),
        in_specs=[smem(), whole, whole, gate, gate, pl.BlockSpec((1, GCH), lambda i: (0, 0))],
        out_specs=pl.BlockSpec((PAIR, GCH), lambda i: (0, 0)),
        scratch_shapes=[pltpu.VMEM((PAIR, GCH), bf16), pltpu.VMEM((PAIR, GCH), bf16)],
        cost_estimate=pl.CostEstimate(flops=1 << 23, bytes_accessed=4 * MIB, transcendentals=1 << 19),
        compiler_params=params(24),
        name="norm",
    )(at, scanned, scanned_other, mine, other, norm_gain)

    shares = []
    for k in (2, 1, 3):
        block = (((tp + k) % T) * C + core).astype(jnp.int32).reshape(1)
        part = project(block, normed, weight, bf16)
        shares.append(lax.ppermute(part, "tp", [(i, (i + k) % T) for i in range(T)]))
    own = project((tp * C + core).astype(jnp.int32).reshape(1), normed, weight, f32)
    keep, away = pl.pallas_call(
        add_kernel,
        out_shape=(shape(ROWS, BLOCK), shape(ROWS, BLOCK)),
        in_specs=[smem()] + [vmem()] * 4,
        out_specs=(vmem(), vmem()),
        compiler_params=params(16),
        name="add",
    )(at, own, *shares)
    got_half = lax.ppermute(away, "c", swap)
    return pl.pallas_call(
        join_kernel,
        out_shape=shape(ROWS, C * BLOCK),
        in_specs=[smem(), vmem(), vmem()],
        out_specs=vmem(),
        compiler_params=params(16),
        name="join",
    )(at, keep, got_half)


def solution(mesh):
    chips = Mesh(mesh.devices.reshape(Z, Y, C, T), ("z", "y", "c", "tp"))
    ctx = ("z", "y", "c")
    return jax.shard_map(
        on_device,
        mesh=chips,
        in_specs=(
            P(ctx, "tp", None),
            P("tp", None, None),
            P("tp", None),
            P("tp", None),
            P("tp", None),
            P("tp", None),
            P("tp", ctx, None),
        ),
        out_specs=P(ctx, "tp"),
        check_vma=False,
    )
```

```python
import jax
import jax.numpy as jnp
from jax import lax
from jax.experimental import pallas as pl
from jax.experimental.pallas import tpu as pltpu
from jax.sharding import Mesh
from jax.sharding import PartitionSpec as P

P_SIZE = 64
N = 256
KCONV = 4
ROWS = 128
PAIR = 256
GCH = 2048
GCONV = 2560
GCOLS = 4640
HALF = 1024
HEADS = 16
BLOCK = 512
Z, Y, C, T = 8, 4, 2, 4
CHIPS = Z * Y
f32, bf16 = jnp.float32, jnp.bfloat16
MIB = 1 << 20


def params(mib):
    return pltpu.CompilerParams(vmem_limit_bytes=mib * MIB)


def vmem():
    return pl.BlockSpec(memory_space=pltpu.VMEM)


def smem():
    return pl.BlockSpec(memory_space=pltpu.SMEM)


def dot(a, b, ca=1, cb=0, precision=None):
    return lax.dot_general(
        a, b, (((ca,), (cb,)), ((), ())), precision=precision, preferred_element_type=f32
    )


def lanes(shape):
    return lax.broadcasted_iota(jnp.int32, shape, 1)


def split_three(v):
    v = jnp.where(lanes(v.shape) < HEADS, v, 0.0)
    high = v.astype(bf16).astype(f32)
    rest = v - high
    middle = rest.astype(bf16).astype(f32)
    low = (rest - middle).astype(bf16).astype(f32)
    packed = high + pltpu.roll(middle, HEADS, 1) + pltpu.roll(low, 2 * HEADS, 1)
    return packed.astype(bf16)


def head_table(first, width):
    row = lax.broadcasted_iota(jnp.int32, (128, width), 0)
    column = lax.broadcasted_iota(jnp.int32, (128, width), 1) + first
    hit = (row < 3 * HEADS) & ((row % HEADS) == column // P_SIZE)
    return jnp.where(hit, 1.0, 0.0).astype(bf16)


def scan_kernel(
    at, mine, other, rim, taps, bias, step_bias, log_rates,
    within, keys, growth, send,
    padded, tap_rows, values, queries, raw, small,
):
    core = at[0]
    x_at = pl.multiple_of(core * HALF, 128)
    mine_at = pl.multiple_of(core * ROWS, 128)
    other_at = pl.multiple_of((1 - core) * ROWS, 128)
    padded[0:8, 0:HALF] = rim[:, pl.ds(x_at, HALF)].astype(f32)
    padded[0:8, HALF:] = rim[:, GCH:GCONV].astype(f32)
    z_end = pl.multiple_of(GCH + x_at, 128)
    for rows, ref in ((mine_at, mine), (other_at, other)):
        target = pl.ds(pl.multiple_of(8 + rows, 8), ROWS)
        padded[target, 0:HALF] = ref[:, pl.ds(z_end, HALF)].astype(f32)
        padded[target, HALF:] = ref[:, 2 * GCH : GCH + GCONV].astype(f32)
        raw[pl.ds(rows, ROWS), :] = jnp.zeros((ROWS, 128), f32)
        raw[pl.ds(rows, ROWS), 0:32] = ref[:, GCH + GCONV : GCOLS].astype(f32)
    tap_rows[0:KCONV, 0:HALF] = taps[:, pl.ds(x_at, HALF)]
    tap_rows[0:KCONV, HALF:] = taps[:, GCH:GCONV]
    tap_rows[4:5, 0:HALF] = bias[:, pl.ds(x_at, HALF)]
    tap_rows[4:5, HALF:] = bias[:, GCH:GCONV]
    small[...] = jnp.zeros((8, 128), f32)
    small[0:1, 0:32] = step_bias[...]
    small[1:2, 0:32] = log_rates[...]

    for c0 in range(0, HALF + 2 * N, 256):
        for r0 in range(0, PAIR, 64):
            total = jnp.broadcast_to(tap_rows[4:5, c0 : c0 + 256], (64, 256))
            for k in range(KCONV):
                total = total + tap_rows[k : k + 1, c0 : c0 + 256] * padded[
                    5 + k + r0 : 5 + k + r0 + 64, c0 : c0 + 256
                ]
            active = (total * jax.nn.sigmoid(total)).astype(bf16)
            if c0 < HALF:
                values[r0 : r0 + 64, c0 : c0 + 256] = active
            elif c0 == HALF:
                keys[r0 : r0 + 64, :] = active
            else:
                queries[r0 : r0 + 64, :] = active

    first = core == 0

    def own(v):
        return jnp.where(first, v, pltpu.roll(v, 128 - HEADS, 1))

    head_lane = lanes((PAIR, 128)) < HEADS
    steps = own(raw[...] + small[0:1, :])
    steps = jnp.where(head_lane, jax.nn.softplus(steps), 0.0)
    rate = -jnp.exp(own(jnp.broadcast_to(small[1:2, :], (8, 128))))[0:1]
    logs = steps * rate
    row = lax.broadcasted_iota(jnp.int32, (PAIR, PAIR), 0)
    column = lax.broadcasted_iota(jnp.int32, (PAIR, PAIR), 1)
    running = dot(jnp.where(row >= column, 1.0, 0.0), logs, precision=lax.Precision.HIGHEST)
    running_t = running.T
    steps_t = steps.T
    growth[...] = split_three(jnp.exp(running))

    causal = row[:ROWS, :ROWS] >= column[:ROWS, :ROWS]
    products = []
    for a in (0, ROWS):
        own_product = dot(queries[a : a + ROWS, :], keys[a : a + ROWS, :], 1, 1)
        products.append(jnp.where(causal, own_product, 0.0))
    across = dot(queries[ROWS:, :], keys[:ROWS, :], 1, 1).astype(bf16)
    low_lane = lanes((ROWS, 128)) < P_SIZE
    for pair in range(HEADS // 2):
        c0 = pair * 128
        for i, a in enumerate((0, ROWS)):
            x = values[a : a + ROWS, c0 : c0 + 128]
            parts = []
            for h in (2 * pair, 2 * pair + 1):
                gap = running[a : a + ROWS, h : h + 1] - running_t[h : h + 1, a : a + ROWS]
                factor = products[i] * jnp.exp(jnp.minimum(gap, 0.0)) * steps_t[h : h + 1, a : a + ROWS]
                parts.append(dot(factor.astype(bf16), x))
            within[a : a + ROWS, c0 : c0 + 128] = jnp.where(low_lane, parts[0], parts[1])

    middle = running[ROWS - 1 : ROWS, :]
    end = running[PAIR - 1 : PAIR, :]
    to_end = split_three(jnp.exp(end - running) * steps)
    to_middle = split_three(jnp.exp(middle - running[:ROWS]) * steps[:ROWS])
    from_middle = split_three(jnp.exp(running[ROWS:] - middle))
    all_logs = split_three(jnp.broadcast_to(end, (PAIR, 128)))
    keys_t = keys[...].astype(f32).T.astype(bf16)
    for c0 in range(0, HALF, 256):
        table = head_table(c0, 256)
        x = values[:, c0 : c0 + 256].astype(f32)
        entering = dot(across, (x[:ROWS] * dot(to_middle, table)).astype(bf16))
        within[ROWS:, c0 : c0 + 256] += entering * dot(from_middle, table)
        weighted = (x * dot(to_end, table)).astype(bf16)
        send[:, c0 : c0 + 256] = dot(keys_t, weighted).astype(bf16)
    send[:, HALF:] = all_logs
    keys[...] = queries[...]


def prefix_kernel(got, back, decays):
    for c0 in range(0, HALF, 256):
        decays[:, c0 : c0 + 256] = jnp.exp(dot(got[:, HALF:], head_table(c0, 256)))
    state = jnp.zeros((8, HALF), f32)
    for pair in range(CHIPS // 2):
        rows = slice(16 * pair, 16 * pair + 16)
        local = got[rows, 0:HALF].astype(f32)
        decay = decays[rows, :]
        second = state * decay[:8] + local[:8]
        back[rows, :] = jnp.concatenate([state, second], axis=0).astype(bf16)
        state = second * decay[8:] + local[8:]


def carried_kernel(within, queries, growth, state, scanned):
    for c0 in range(0, HALF, 256):
        carried = dot(queries[...], state[:, c0 : c0 + 256])
        carried = carried * dot(growth[...], head_table(c0, 256))
        scanned[:, c0 : c0 + 256] = (within[:, c0 : c0 + 256] + carried).astype(bf16)


def norm_kernel(at, scanned, scanned_other, gate, gate_other, gain, normed, whole, gates):
    core = at[0]
    own_at = pl.multiple_of(core * HALF, 128)
    other_at = pl.multiple_of((1 - core) * HALF, 128)
    whole[:, pl.ds(own_at, HALF)] = scanned[...]
    whole[:, pl.ds(other_at, HALF)] = scanned_other[...]
    gates[pl.ds(pl.multiple_of(core * ROWS, 128), ROWS), :] = gate[:, 0:GCH]
    gates[pl.ds(pl.multiple_of((1 - core) * ROWS, 128), ROWS), :] = gate_other[:, 0:GCH]

    def body(i, carry):
        rows = pl.ds(pl.multiple_of(i * 16, 16), 16)
        g = gates[rows, :].astype(f32)
        gated = whole[rows, :].astype(f32) * (g * jax.nn.sigmoid(g))
        scale = lax.rsqrt(jnp.mean(gated * gated, axis=1, keepdims=True) + 1e-05)
        normed[rows, :] = (gated * scale * gain[...]).astype(bf16)
        return carry

    lax.fori_loop(0, PAIR // 16, body, 0)


def project_kernel(at, normed, weight, out, total):
    step = pl.program_id(0)

    @pl.when(step == 0)
    def _():
        total[...] = jnp.zeros_like(total)

    total[...] += dot(normed[...], weight[...])

    @pl.when(step == pl.num_programs(0) - 1)
    def _():
        out[...] = total[...].astype(out.dtype)


def project(block, normed, weight, dtype):
    depth = 512
    return pl.pallas_call(
        project_kernel,
        out_shape=jax.ShapeDtypeStruct((PAIR, BLOCK), dtype),
        grid_spec=pltpu.PrefetchScalarGridSpec(
            num_scalar_prefetch=1,
            grid=(GCH // depth,),
            in_specs=[
                pl.BlockSpec((PAIR, depth), lambda k, at: (0, k)),
                pl.BlockSpec((depth, BLOCK), lambda k, at: (k, at[0])),
            ],
            out_specs=pl.BlockSpec((PAIR, BLOCK), lambda k, at: (0, 0)),
            scratch_shapes=[pltpu.VMEM((PAIR, BLOCK), f32)],
        ),
        cost_estimate=pl.CostEstimate(
            flops=2 * PAIR * GCH * BLOCK, bytes_accessed=2 * GCH * BLOCK, transcendentals=0
        ),
        compiler_params=params(52),
        name="project",
    )(block, normed, weight)


def add_kernel(at, own, a, b, c, keep, away):
    core = at[0]
    for ref, which in ((keep, core), (away, 1 - core)):
        rows = pl.ds(pl.multiple_of(which * ROWS, 128), ROWS)
        total = own[rows, :] + a[rows, :].astype(f32) + b[rows, :].astype(f32)
        ref[...] = (total + c[rows, :].astype(f32)).astype(bf16)


def join_kernel(at, keep, got, out):
    core = at[0]
    out[:, pl.ds(pl.multiple_of(core * BLOCK, 128), BLOCK)] = keep[...]
    out[:, pl.ds(pl.multiple_of((1 - core) * BLOCK, 128), BLOCK)] = got[...]


def shape(*dims, dtype=bf16):
    return jax.ShapeDtypeStruct(dims, dtype)


def on_device(projected, conv_weight, conv_bias, step_bias, log_rates, norm_gain, out_weight):
    weight = lax.all_gather(out_weight[0], ("z", "y", "c"), axis=0, tiled=True)
    mine = projected.reshape(ROWS, GCOLS)
    swap = [(0, 1), (1, 0)]
    other = lax.ppermute(mine, "c", swap)
    tail = mine[ROWS - 8 :, GCH : GCH + GCONV]
    all_axes = ("z", "y", "c")
    rim_0 = lax.ppermute(tail, all_axes, [(2 * i + 1, 2 * i + 2) for i in range(CHIPS - 1)])
    rim_1 = lax.ppermute(tail, all_axes, [(2 * i + 1, 2 * i + 3) for i in range(CHIPS - 1)])
    core, tp = lax.axis_index("c"), lax.axis_index("tp")
    rim = jnp.where(core == 0, rim_0, rim_1)
    at = core.astype(jnp.int32).reshape(1)

    within, queries, growth, send = pl.pallas_call(
        scan_kernel,
        out_shape=(
            shape(PAIR, HALF, dtype=f32), shape(PAIR, N), shape(PAIR, 128), shape(N, HALF + 128),
        ),
        in_specs=[smem()] + [vmem()] * 7,
        out_specs=(vmem(),) * 4,
        scratch_shapes=[
            pltpu.VMEM((PAIR + 8, HALF + 2 * N), f32),
            pltpu.VMEM((8, HALF + 2 * N), f32),
            pltpu.VMEM((PAIR, HALF), bf16),
            pltpu.VMEM((PAIR, N), bf16),
            pltpu.VMEM((PAIR, 128), f32),
            pltpu.VMEM((8, 128), f32),
        ],
        cost_estimate=pl.CostEstimate(
            flops=1 << 29, bytes_accessed=5 * MIB, transcendentals=1 << 20
        ),
        compiler_params=params(32),
        name="scan",
    )(at, mine, other, rim, conv_weight[0], conv_bias, step_bias, log_rates)

    got = lax.all_to_all(send, ("z", "y"), 0, 0, tiled=True)
    back = pl.pallas_call(
        prefix_kernel,
        out_shape=shape(N, HALF),
        in_specs=[vmem()],
        out_specs=vmem(),
        scratch_shapes=[pltpu.VMEM((N, HALF), f32)],
        cost_estimate=pl.CostEstimate(flops=1 << 26, bytes_accessed=MIB, transcendentals=1 << 18),
        compiler_params=params(16),
        name="prefix",
    )(got)
    state = lax.all_to_all(back, ("z", "y"), 0, 0, tiled=True)
    scanned = pl.pallas_call(
        carried_kernel,
        out_shape=shape(PAIR, HALF),
        in_specs=[vmem()] * 4,
        out_specs=vmem(),
        cost_estimate=pl.CostEstimate(flops=1 << 28, bytes_accessed=2 * MIB, transcendentals=0),
        compiler_params=params(16),
        name="carried",
    )(within, queries, growth, state)
    scanned_other = lax.ppermute(scanned, "c", swap)

    normed = pl.pallas_call(
        norm_kernel,
        out_shape=shape(PAIR, GCH),
        in_specs=[smem()] + [vmem()] * 5,
        out_specs=vmem(),
        scratch_shapes=[pltpu.VMEM((PAIR, GCH), bf16), pltpu.VMEM((PAIR, GCH), bf16)],
        cost_estimate=pl.CostEstimate(flops=1 << 23, bytes_accessed=4 * MIB, transcendentals=1 << 19),
        compiler_params=params(24),
        name="norm",
    )(at, scanned, scanned_other, mine, other, norm_gain)

    shares = []
    for k in (2, 1, 3):
        block = (((tp + k) % T) * C + core).astype(jnp.int32).reshape(1)
        part = project(block, normed, weight, bf16)
        shares.append(lax.ppermute(part, "tp", [(i, (i + k) % T) for i in range(T)]))
    own = project((tp * C + core).astype(jnp.int32).reshape(1), normed, weight, f32)
    keep, away = pl.pallas_call(
        add_kernel,
        out_shape=(shape(ROWS, BLOCK), shape(ROWS, BLOCK)),
        in_specs=[smem()] + [vmem()] * 4,
        out_specs=(vmem(), vmem()),
        compiler_params=params(16),
        name="add",
    )(at, own, *shares)
    got_half = lax.ppermute(away, "c", swap)
    return pl.pallas_call(
        join_kernel,
        out_shape=shape(ROWS, C * BLOCK),
        in_specs=[smem(), vmem(), vmem()],
        out_specs=vmem(),
        compiler_params=params(16),
        name="join",
    )(at, keep, got_half)


def solution(mesh):
    chips = Mesh(mesh.devices.reshape(Z, Y, C, T), ("z", "y", "c", "tp"))
    ctx = ("z", "y", "c")
    return jax.shard_map(
        on_device,
        mesh=chips,
        in_specs=(
            P(ctx, "tp", None),
            P("tp", None, None),
            P("tp", None),
            P("tp", None),
            P("tp", None),
            P("tp", None),
            P("tp", ctx, None),
        ),
        out_specs=P(ctx, "tp"),
        check_vma=False,
    )
```

```python
import functools

import jax
import jax.numpy as jnp
from jax import lax
from jax.experimental import pallas as pl
from jax.experimental.pallas import tpu as pltpu
from jax.sharding import Mesh
from jax.sharding import PartitionSpec as P

P_SIZE = 64
N = 256
KCONV = 4
ROWS = 128
PAIR = 256
QUAD = 512
GCH = 2048
GCONV = 2560
GCOLS = 4640
HALF = 1024
HEADS = 16
BLOCK = 256
Z, Y, C, T = 8, 4, 2, 4
CHIPS = Z * Y
f32, bf16 = jnp.float32, jnp.bfloat16
MIB = 1 << 20
QUERY, GROWTH, STATE, LOGS = 1024, 1280, 1408, 2432
PACK = 2560


def params(mib):
    return pltpu.CompilerParams(vmem_limit_bytes=mib * MIB)


def vmem():
    return pl.BlockSpec(memory_space=pltpu.VMEM)


def smem():
    return pl.BlockSpec(memory_space=pltpu.SMEM)


def dot(a, b, ca=1, cb=0, precision=None):
    return lax.dot_general(
        a, b, (((ca,), (cb,)), ((), ())), precision=precision, preferred_element_type=f32
    )


def lanes(shape):
    return lax.broadcasted_iota(jnp.int32, shape, 1)


def split_three(v):
    v = jnp.where(lanes(v.shape) < HEADS, v, 0.0)
    high = v.astype(bf16).astype(f32)
    rest = v - high
    middle = rest.astype(bf16).astype(f32)
    low = (rest - middle).astype(bf16).astype(f32)
    packed = high + pltpu.roll(middle, HEADS, 1) + pltpu.roll(low, 2 * HEADS, 1)
    return packed.astype(bf16)


def head_table(first, width):
    row = lax.broadcasted_iota(jnp.int32, (128, width), 0)
    column = lax.broadcasted_iota(jnp.int32, (128, width), 1) + first
    hit = (row < 3 * HEADS) & ((row % HEADS) == column // P_SIZE)
    return jnp.where(hit, 1.0, 0.0).astype(bf16)


def scan_kernel(
    at, mine, other, rim, taps, bias, step_bias, log_rates,
    pack, send,
    within, keys, padded, tap_rows, values, queries, raw, small,
):
    core = at[0]
    x_at = pl.multiple_of(core * HALF, 128)
    mine_at = pl.multiple_of(core * ROWS, 128)
    other_at = pl.multiple_of((1 - core) * ROWS, 128)
    padded[0:8, 0:HALF] = rim[:, pl.ds(x_at, HALF)].astype(f32)
    padded[0:8, HALF:] = rim[:, GCH:GCONV].astype(f32)
    z_end = pl.multiple_of(GCH + x_at, 128)
    for rows, ref in ((mine_at, mine), (other_at, other)):
        target = pl.ds(pl.multiple_of(8 + rows, 8), ROWS)
        padded[target, 0:HALF] = ref[:, pl.ds(z_end, HALF)].astype(f32)
        padded[target, HALF:] = ref[:, 2 * GCH : GCH + GCONV].astype(f32)
        raw[pl.ds(rows, ROWS), :] = jnp.zeros((ROWS, 128), f32)
        raw[pl.ds(rows, ROWS), 0:32] = ref[:, GCH + GCONV : GCOLS].astype(f32)
    tap_rows[0:KCONV, 0:HALF] = taps[:, pl.ds(x_at, HALF)]
    tap_rows[0:KCONV, HALF:] = taps[:, GCH:GCONV]
    tap_rows[4:5, 0:HALF] = bias[:, pl.ds(x_at, HALF)]
    tap_rows[4:5, HALF:] = bias[:, GCH:GCONV]
    small[...] = jnp.zeros((8, 128), f32)
    small[0:1, 0:32] = step_bias[...]
    small[1:2, 0:32] = log_rates[...]

    for c0 in range(0, HALF + 2 * N, 256):
        for r0 in range(0, PAIR, 64):
            total = jnp.broadcast_to(tap_rows[4:5, c0 : c0 + 256], (64, 256))
            for k in range(KCONV):
                total = total + tap_rows[k : k + 1, c0 : c0 + 256] * padded[
                    5 + k + r0 : 5 + k + r0 + 64, c0 : c0 + 256
                ]
            active = (total * jax.nn.sigmoid(total)).astype(bf16)
            if c0 < HALF:
                values[r0 : r0 + 64, c0 : c0 + 256] = active
            elif c0 == HALF:
                keys[r0 : r0 + 64, :] = active
            else:
                queries[r0 : r0 + 64, :] = active

    first = core == 0

    def own(v):
        return jnp.where(first, v, pltpu.roll(v, 128 - HEADS, 1))

    head_lane = lanes((PAIR, 128)) < HEADS
    steps = own(raw[...] + small[0:1, :])
    steps = jnp.where(head_lane, jax.nn.softplus(steps), 0.0)
    rate = -jnp.exp(own(jnp.broadcast_to(small[1:2, :], (8, 128))))[0:1]
    logs = steps * rate
    row = lax.broadcasted_iota(jnp.int32, (PAIR, PAIR), 0)
    column = lax.broadcasted_iota(jnp.int32, (PAIR, PAIR), 1)
    running = dot(jnp.where(row >= column, 1.0, 0.0), logs, precision=lax.Precision.HIGHEST)
    running_t = running.T
    steps_t = steps.T
    pack[:, GROWTH : GROWTH + 128] = split_three(jnp.exp(running))

    causal = row[:ROWS, :ROWS] >= column[:ROWS, :ROWS]
    products = []
    for a in (0, ROWS):
        own_product = dot(queries[a : a + ROWS, :], keys[a : a + ROWS, :], 1, 1)
        products.append(jnp.where(causal, own_product, 0.0))
    across = dot(queries[ROWS:, :], keys[:ROWS, :], 1, 1).astype(bf16)
    low_lane = lanes((ROWS, 128)) < P_SIZE
    for pair in range(HEADS // 2):
        c0 = pair * 128
        for i, a in enumerate((0, ROWS)):
            x = values[a : a + ROWS, c0 : c0 + 128]
            parts = []
            for h in (2 * pair, 2 * pair + 1):
                gap = running[a : a + ROWS, h : h + 1] - running_t[h : h + 1, a : a + ROWS]
                factor = products[i] * jnp.exp(jnp.minimum(gap, 0.0)) * steps_t[h : h + 1, a : a + ROWS]
                parts.append(dot(factor.astype(bf16), x))
            within[a : a + ROWS, c0 : c0 + 128] = jnp.where(low_lane, parts[0], parts[1])

    middle = running[ROWS - 1 : ROWS, :]
    end = running[PAIR - 1 : PAIR, :]
    to_end = split_three(jnp.exp(end - running) * steps)
    to_middle = split_three(jnp.exp(middle - running[:ROWS]) * steps[:ROWS])
    from_middle = split_three(jnp.exp(running[ROWS:] - middle))
    all_logs = split_three(jnp.broadcast_to(end, (PAIR, 128)))
    keys_t = keys[...].astype(f32).T.astype(bf16)
    for c0 in range(0, HALF, 256):
        table = head_table(c0, 256)
        x = values[:, c0 : c0 + 256].astype(f32)
        entering = dot(across, (x[:ROWS] * dot(to_middle, table)).astype(bf16))
        within[ROWS:, c0 : c0 + 256] += entering * dot(from_middle, table)
        weighted = (x * dot(to_end, table)).astype(bf16)
        send[:, c0 : c0 + 256] = dot(keys_t, weighted).astype(bf16)
        pack[:, c0 : c0 + 256] = within[:, c0 : c0 + 256].astype(bf16)
    send[:, HALF:] = all_logs
    pack[:, STATE:] = send[...]
    pack[:, QUERY : QUERY + N] = queries[...]


def prefix_kernel(got, back, decays):
    for c0 in range(0, HALF, 256):
        decays[:, c0 : c0 + 256] = jnp.exp(dot(got[:, HALF:], head_table(c0, 256)))
    state = jnp.zeros((8, HALF), f32)
    for pair in range(CHIPS // 2):
        rows = slice(16 * pair, 16 * pair + 16)
        local = got[rows, 0:HALF].astype(f32)
        decay = decays[rows, :]
        second = state * decay[:8] + local[:8]
        back[rows, :] = jnp.concatenate([state, state], axis=0).astype(bf16)
        state = second * decay[8:] + local[8:]


def carried_kernel(at, own, got, own_gate, got_gate, state, gated, packs, gates):
    gates[lax.rem(at[1], 2)] = own_gate[...]
    gates[lax.rem(at[1] + 1, 2)] = got_gate[...]
    packs[lax.rem(at[1], 2)] = own[...]
    packs[lax.rem(at[1] + 1, 2)] = got[...]
    for c0 in range(0, HALF, 256):
        table = head_table(c0, 256)
        first = state[:, c0 : c0 + 256]
        decay = jnp.exp(dot(packs[0, 0:16, LOGS:], table)[0:1])
        second = first.astype(f32) * decay
        second = second + packs[0, :, STATE + c0 : STATE + c0 + 256].astype(f32)
        for i, before in ((0, first), (1, second.astype(bf16))):
            carried = dot(packs[i, :, QUERY : QUERY + N], before)
            carried = carried * dot(packs[i, :, GROWTH : GROWTH + 128], table)
            scanned = (packs[i, :, c0 : c0 + 256].astype(f32) + carried).astype(bf16)
            g = gates[i, :, c0 : c0 + 256].astype(f32)
            result = scanned.astype(f32) * (g * jax.nn.sigmoid(g))
            gated[i * PAIR : (i + 1) * PAIR, c0 : c0 + 256] = result.astype(bf16)


def norm_kernel(at, own, got, gain, normed, whole):
    core = at[0]
    whole[:, pl.ds(pl.multiple_of(core * HALF, 128), HALF)] = own[...]
    whole[:, pl.ds(pl.multiple_of((1 - core) * HALF, 128), HALF)] = got[...]

    def body(i, carry):
        rows = pl.ds(pl.multiple_of(i * 32, 32), 32)
        gated = whole[rows, :].astype(f32)
        scale = lax.rsqrt(jnp.mean(gated * gated, axis=1, keepdims=True) + 1e-05)
        normed[rows, :] = (gated * scale * gain[...]).astype(bf16)
        return carry

    lax.fori_loop(0, QUAD // 32, body, 0)


def gate_kernel(at, mine, other, gate):
    core = at[0]
    columns = pl.ds(pl.multiple_of(core * HALF, 128), HALF)
    gate[pl.ds(pl.multiple_of(core * ROWS, 128), ROWS), :] = mine[:, columns]
    gate[pl.ds(pl.multiple_of((1 - core) * ROWS, 128), ROWS), :] = other[:, columns]


def pick_kernel(at, weight, own, away):
    for ref, which in ((own, at[0]), (away, 1 - at[0])):
        for chip in range(2):
            for j in range(T):
                source = pl.multiple_of((j * 4 + chip * 2 + which) * BLOCK, 128)
                ref[chip, :, j * BLOCK : (j + 1) * BLOCK] = weight[:, pl.ds(source, BLOCK)]


def stack_kernel(at, own, got, near, far):
    chip = lax.rem(at[1], 2)
    for ref, which in ((own, at[0]), (got, 1 - at[0])):
        rows = pl.ds(pl.multiple_of(which * 32, 32), 32)
        near[rows, :] = ref[chip]
        far[rows, :] = ref[1 - chip]


def order_kernel(at, *refs):
    out = refs[-1]
    for m, part in enumerate(refs[:-1]):
        rows = pl.ds(pl.multiple_of(jnp.bitwise_xor(at[1], m) * 64, 64), 64)
        for j in range(T):
            out[j, rows, :] = part[:, j * BLOCK : (j + 1) * BLOCK]


def project_kernel(at, normed, lower, upper, *outs):
    total = jnp.zeros((QUAD, BLOCK), f32)
    for z in range(Z):
        block = lower[z, 0] if z < Z // 2 else upper[z - Z // 2, 0]
        total = total + dot(normed[:, z * 256 : (z + 1) * 256], block)
    for i, out in enumerate(outs):

        @pl.when(pl.program_id(0) == i)
        def _(out=out):
            out[...] = total.astype(out.dtype)


def project(blocks, normed, weight, dtype):
    count = blocks.shape[0]

    def all_of(i, at):
        return (0, 0)

    return pl.pallas_call(
        project_kernel,
        out_shape=(shape(QUAD, BLOCK, dtype=dtype),) * count,
        grid_spec=pltpu.PrefetchScalarGridSpec(
            num_scalar_prefetch=1,
            grid=(count,),
            in_specs=[
                pl.BlockSpec((QUAD, GCH), all_of),
                pl.BlockSpec((Z // 2, 1, 256, BLOCK), lambda i, at: (0, at[i], 0, 0)),
                pl.BlockSpec((Z // 2, 1, 256, BLOCK), lambda i, at: (1, at[i], 0, 0)),
            ],
            out_specs=[pl.BlockSpec((QUAD, BLOCK), all_of)] * count,
        ),
        cost_estimate=pl.CostEstimate(
            flops=2 * QUAD * GCH * BLOCK * count,
            bytes_accessed=2 * GCH * BLOCK * count,
            transcendentals=0,
        ),
        compiler_params=params(52),
        name="project",
    )(blocks, normed, weight, weight)


def add_kernel(at, own, a, b, c, *parts):
    for m, part in enumerate(parts):
        which = lax.rem(jnp.bitwise_xor(at[2], m), 4)
        rows = pl.ds(pl.multiple_of(which * ROWS, 128), ROWS)
        total = own[rows, :] + a[rows, :].astype(f32) + b[rows, :].astype(f32)
        part[...] = (total + c[rows, :].astype(f32)).astype(bf16)


def join_kernel(at, *refs):
    out = refs[-1]
    for m, part in enumerate(refs[:-1]):
        which = lax.rem(jnp.bitwise_xor(at[2], m), 4)
        out[:, pl.ds(pl.multiple_of(which * BLOCK, 128), BLOCK)] = part[...]


def flip(block, m):
    return lax.ppermute(block, ("y", "c"), [(i, i ^ m) for i in range(Y * C)])


def together(*groups):
    return lax.optimization_barrier(groups)


def shape(*dims, dtype=bf16):
    return jax.ShapeDtypeStruct(dims, dtype)


def on_device(projected, conv_weight, conv_bias, step_bias, log_rates, norm_gain, out_weight):
    core, y, tp = (lax.axis_index(name) for name in ("c", "y", "tp"))
    at = jnp.stack([core, y, y * C + core]).astype(jnp.int32)
    mine = projected.reshape(ROWS, GCOLS)
    swap = [(0, 1), (1, 0)]
    other = lax.ppermute(mine, "c", swap)
    tail = mine[ROWS - 8 :, GCH : GCH + GCONV]
    all_axes = ("z", "y", "c")
    rim_0 = lax.ppermute(tail, all_axes, [(2 * i + 1, 2 * i + 2) for i in range(CHIPS - 1)])
    rim_1 = lax.ppermute(tail, all_axes, [(2 * i + 1, 2 * i + 3) for i in range(CHIPS - 1)])
    rim = jnp.where(core == 0, rim_0, rim_1)
    own, away = pl.pallas_call(
        pick_kernel,
        out_shape=(shape(2, 32, T * BLOCK),) * 2,
        in_specs=[smem(), vmem()],
        out_specs=(vmem(),) * 2,
        compiler_params=params(8),
        name="pick",
    )(at, out_weight[0])
    near, far = pl.pallas_call(
        stack_kernel,
        out_shape=(shape(64, T * BLOCK),) * 2,
        in_specs=[smem(), vmem(), vmem()],
        out_specs=(vmem(),) * 2,
        compiler_params=params(8),
        name="stack",
    )(at, own, lax.ppermute(away, "c", swap))
    plane_weight = pl.pallas_call(
        order_kernel,
        out_shape=shape(T, 256, BLOCK),
        in_specs=[smem()] + [vmem()] * 4,
        out_specs=vmem(),
        compiler_params=params(8),
        name="order",
    )(at, near, flip(far, 2), flip(near, 4), flip(far, 6))
    gate = pl.pallas_call(
        gate_kernel,
        out_shape=shape(PAIR, HALF),
        in_specs=[smem(), vmem(), vmem()],
        out_specs=vmem(),
        compiler_params=params(8),
        name="gate",
    )(at, mine, other)
    gate, other, rim = together(gate, other, rim)
    got_gate = flip(gate, 2)

    pack, send = pl.pallas_call(
        scan_kernel,
        out_shape=(shape(PAIR, PACK), shape(N, HALF + 128)),
        in_specs=[smem()] + [vmem()] * 7,
        out_specs=(vmem(),) * 2,
        scratch_shapes=[
            pltpu.VMEM((PAIR, HALF), f32),
            pltpu.VMEM((PAIR, N), bf16),
            pltpu.VMEM((PAIR + 8, HALF + 2 * N), f32),
            pltpu.VMEM((8, HALF + 2 * N), f32),
            pltpu.VMEM((PAIR, HALF), bf16),
            pltpu.VMEM((PAIR, N), bf16),
            pltpu.VMEM((PAIR, 128), f32),
            pltpu.VMEM((8, 128), f32),
        ],
        cost_estimate=pl.CostEstimate(
            flops=1 << 29, bytes_accessed=5 * MIB, transcendentals=1 << 20
        ),
        compiler_params=params(20),
        name="scan",
    )(at, mine, other, rim, conv_weight[0], conv_bias, step_bias, log_rates)

    plane_weight, send, pack, got_gate = together(plane_weight, send, pack, got_gate)
    weight = lax.all_gather(plane_weight.reshape(T * 256, BLOCK), "z", axis=0, tiled=True)
    weight = weight.reshape(Z, T, 256, BLOCK)
    got_pack = flip(pack, 2)
    got = lax.all_to_all(send, ("z", "y"), 0, 0, tiled=True)
    back = pl.pallas_call(
        prefix_kernel,
        out_shape=shape(N, HALF),
        in_specs=[vmem()],
        out_specs=vmem(),
        scratch_shapes=[pltpu.VMEM((N, HALF), f32)],
        cost_estimate=pl.CostEstimate(flops=1 << 26, bytes_accessed=MIB, transcendentals=1 << 18),
        compiler_params=params(16),
        name="prefix",
    )(got)
    state = lax.all_to_all(back, ("z", "y"), 0, 0, tiled=True)
    gated = pl.pallas_call(
        carried_kernel,
        out_shape=shape(QUAD, HALF),
        in_specs=[smem()] + [vmem()] * 5,
        out_specs=vmem(),
        scratch_shapes=[pltpu.VMEM((2, PAIR, PACK), bf16), pltpu.VMEM((2, PAIR, HALF), bf16)],
        cost_estimate=pl.CostEstimate(flops=1 << 29, bytes_accessed=4 * MIB, transcendentals=1 << 19),
        compiler_params=params(16),
        name="carried",
    )(at, pack, got_pack, gate, got_gate, state)
    normed = pl.pallas_call(
        norm_kernel,
        out_shape=shape(QUAD, GCH),
        in_specs=[smem()] + [vmem()] * 3,
        out_specs=vmem(),
        scratch_shapes=[pltpu.VMEM((QUAD, GCH), bf16)],
        cost_estimate=pl.CostEstimate(flops=1 << 23, bytes_accessed=4 * MIB, transcendentals=0),
        compiler_params=params(12),
        name="norm",
    )(at, gated, lax.ppermute(gated, "c", swap), norm_gain)

    offsets = (2, 1, 3)
    blocks = lax.rem(tp + jnp.asarray(offsets + (0,), jnp.int32), T).astype(jnp.int32)
    shares = [
        lax.ppermute(part, "tp", [(i, (i + k) % T) for i in range(T)])
        for k, part in zip(offsets, project(blocks[:3], normed, weight, bf16), strict=True)
    ]
    (own_share,) = project(blocks[3:], normed, weight, f32)
    parts = pl.pallas_call(
        add_kernel,
        out_shape=(shape(ROWS, BLOCK),) * 4,
        in_specs=[smem()] + [vmem()] * 4,
        out_specs=(vmem(),) * 4,
        compiler_params=params(8),
        name="add",
    )(at, own_share, *shares)
    return pl.pallas_call(
        join_kernel,
        out_shape=shape(ROWS, 4 * BLOCK),
        in_specs=[smem()] + [vmem()] * 4,
        out_specs=vmem(),
        compiler_params=params(8),
        name="join",
    )(at, parts[0], *[flip(parts[m], m) for m in (1, 2, 3)])


def solution(mesh):
    chips = Mesh(mesh.devices.reshape(Z, Y, C, T), ("z", "y", "c", "tp"))
    ctx = ("z", "y", "c")
    return jax.shard_map(
        on_device,
        mesh=chips,
        in_specs=(
            P(ctx, "tp", None),
            P("tp", None, None),
            P("tp", None),
            P("tp", None),
            P("tp", None),
            P("tp", None),
            P("tp", ctx, None),
        ),
        out_specs=P(ctx, "tp"),
        check_vma=False,
    )
```

```python
import functools

import jax
import jax.numpy as jnp
from jax import lax
from jax.experimental import pallas as pl
from jax.experimental.pallas import tpu as pltpu
from jax.sharding import Mesh
from jax.sharding import PartitionSpec as P

P_SIZE = 64
N = 256
KCONV = 4
ROWS = 128
PAIR = 256
GCH = 2048
GCONV = 2560
GCOLS = 4640
HALF = 1024
HEADS = 16
QUARTER = HALF // 4
SLICE = N // 8
BLOCK = 512
Z, Y, C, T = 8, 4, 2, 4
CHIPS = Z * Y
f32, bf16 = jnp.float32, jnp.bfloat16
MIB = 1 << 20


def params(mib):
    return pltpu.CompilerParams(vmem_limit_bytes=mib * MIB)


def vmem():
    return pl.BlockSpec(memory_space=pltpu.VMEM)


def smem():
    return pl.BlockSpec(memory_space=pltpu.SMEM)


def dot(a, b, ca=1, cb=0, precision=None):
    return lax.dot_general(
        a, b, (((ca,), (cb,)), ((), ())), precision=precision, preferred_element_type=f32
    )


def lanes(shape):
    return lax.broadcasted_iota(jnp.int32, shape, 1)


def split_three(v):
    v = jnp.where(lanes(v.shape) < HEADS, v, 0.0)
    high = v.astype(bf16).astype(f32)
    rest = v - high
    middle = rest.astype(bf16).astype(f32)
    low = (rest - middle).astype(bf16).astype(f32)
    packed = high + pltpu.roll(middle, HEADS, 1) + pltpu.roll(low, 2 * HEADS, 1)
    return packed.astype(bf16)


def head_table(first, width):
    row = lax.broadcasted_iota(jnp.int32, (128, width), 0)
    column = lax.broadcasted_iota(jnp.int32, (128, width), 1) + first
    hit = (row < 3 * HEADS) & ((row % HEADS) == column // P_SIZE)
    return jnp.where(hit, 1.0, 0.0).astype(bf16)


def three_rows(v):
    row = lax.broadcasted_iota(jnp.int32, v.shape, 0)
    high = v.astype(bf16).astype(f32)
    middle = (v - high).astype(bf16).astype(f32)
    low = (v - high - middle).astype(bf16).astype(f32)
    picked = jnp.where(row == 0, high, jnp.where(row == 1, middle, jnp.where(row == 2, low, 0.0)))
    return picked.astype(bf16)


def log_row(rows):
    return jnp.sum(rows.astype(f32), axis=0, keepdims=True)


def scan_kernel(
    at, mine, other, rim, taps, bias, step_bias, log_rates,
    within, keys, growth, send_0, send_1, send_2, send_3,
    padded, tap_rows, values, queries, raw, small,
):
    core = at[0]
    x_at = pl.multiple_of(core * HALF, 128)
    mine_at = pl.multiple_of(core * ROWS, 128)
    other_at = pl.multiple_of((1 - core) * ROWS, 128)
    padded[0:8, 0:HALF] = rim[:, pl.ds(x_at, HALF)].astype(f32)
    padded[0:8, HALF:] = rim[:, GCH:GCONV].astype(f32)
    z_end = pl.multiple_of(GCH + x_at, 128)
    for rows, ref in ((mine_at, mine), (other_at, other)):
        target = pl.ds(pl.multiple_of(8 + rows, 8), ROWS)
        padded[target, 0:HALF] = ref[:, pl.ds(z_end, HALF)].astype(f32)
        padded[target, HALF:] = ref[:, 2 * GCH : GCH + GCONV].astype(f32)
        raw[pl.ds(rows, ROWS), :] = jnp.zeros((ROWS, 128), f32)
        raw[pl.ds(rows, ROWS), 0:32] = ref[:, GCH + GCONV : GCOLS].astype(f32)
    tap_rows[0:KCONV, 0:HALF] = taps[:, pl.ds(x_at, HALF)]
    tap_rows[0:KCONV, HALF:] = taps[:, GCH:GCONV]
    tap_rows[4:5, 0:HALF] = bias[:, pl.ds(x_at, HALF)]
    tap_rows[4:5, HALF:] = bias[:, GCH:GCONV]
    small[...] = jnp.zeros((8, 128), f32)
    small[0:1, 0:32] = step_bias[...]
    small[1:2, 0:32] = log_rates[...]

    for c0 in range(0, HALF + 2 * N, 256):
        for r0 in range(0, PAIR, 64):
            total = jnp.broadcast_to(tap_rows[4:5, c0 : c0 + 256], (64, 256))
            for k in range(KCONV):
                total = total + tap_rows[k : k + 1, c0 : c0 + 256] * padded[
                    5 + k + r0 : 5 + k + r0 + 64, c0 : c0 + 256
                ]
            active = (total * jax.nn.sigmoid(total)).astype(bf16)
            if c0 < HALF:
                values[r0 : r0 + 64, c0 : c0 + 256] = active
            elif c0 == HALF:
                keys[r0 : r0 + 64, :] = active
            else:
                queries[r0 : r0 + 64, :] = active

    first = core == 0

    def own(v):
        return jnp.where(first, v, pltpu.roll(v, 128 - HEADS, 1))

    head_lane = lanes((PAIR, 128)) < HEADS
    steps = own(raw[...] + small[0:1, :])
    steps = jnp.where(head_lane, jax.nn.softplus(steps), 0.0)
    rate = -jnp.exp(own(jnp.broadcast_to(small[1:2, :], (8, 128))))[0:1]
    logs = steps * rate
    row = lax.broadcasted_iota(jnp.int32, (PAIR, PAIR), 0)
    column = lax.broadcasted_iota(jnp.int32, (PAIR, PAIR), 1)
    running = dot(jnp.where(row >= column, 1.0, 0.0), logs, precision=lax.Precision.HIGHEST)
    running_t = running.T
    steps_t = steps.T
    growth[...] = split_three(jnp.exp(running))

    causal = row[:ROWS, :ROWS] >= column[:ROWS, :ROWS]
    products = []
    for a in (0, ROWS):
        own_product = dot(queries[a : a + ROWS, :], keys[a : a + ROWS, :], 1, 1)
        products.append(jnp.where(causal, own_product, 0.0))
    across = dot(queries[ROWS:, :], keys[:ROWS, :], 1, 1).astype(bf16)
    low_lane = lanes((ROWS, 128)) < P_SIZE
    for pair in range(HEADS // 2):
        c0 = pair * 128
        for i, a in enumerate((0, ROWS)):
            x = values[a : a + ROWS, c0 : c0 + 128]
            parts = []
            for h in (2 * pair, 2 * pair + 1):
                gap = running[a : a + ROWS, h : h + 1] - running_t[h : h + 1, a : a + ROWS]
                factor = products[i] * jnp.exp(jnp.minimum(gap, 0.0)) * steps_t[h : h + 1, a : a + ROWS]
                parts.append(dot(factor.astype(bf16), x))
            within[a : a + ROWS, c0 : c0 + 128] = jnp.where(low_lane, parts[0], parts[1])

    middle = running[ROWS - 1 : ROWS, :]
    end = running[PAIR - 1 : PAIR, :]
    to_end = split_three(jnp.exp(end - running) * steps)
    to_middle = split_three(jnp.exp(middle - running[:ROWS]) * steps[:ROWS])
    from_middle = split_three(jnp.exp(running[ROWS:] - middle))
    all_logs = split_three(jnp.broadcast_to(end, (16, 128)))
    keys_t = keys[...].astype(f32).T.astype(bf16)
    for k, send in enumerate((send_0, send_1, send_2, send_3)):
        c0 = pl.multiple_of(lax.rem(at[1] + k, Y) * QUARTER, 128)
        columns = pl.ds(c0, QUARTER)
        table = head_table(c0, QUARTER)
        x = values[:, columns].astype(f32)
        entering = dot(across, (x[:ROWS] * dot(to_middle, table)).astype(bf16))
        within[ROWS:, columns] += entering * dot(from_middle, table)
        weighted = (x * dot(to_end, table)).astype(bf16)
        send[0:N, :] = dot(keys_t, weighted).astype(bf16)
        send[N:, :] = three_rows(dot(all_logs, table))
    keys[...] = queries[...]


def in_order(at, parts, ordered):
    for k, part in enumerate(parts):
        ordered[lax.rem(at[1] + (Y - k), Y)] = part[...]


def plane_kernel(at, part_0, part_1, part_2, part_3, send, ordered):
    in_order(at, (part_0, part_1, part_2, part_3), ordered)
    logs = [log_row(ordered[y, N : N + 16, :]) for y in range(Y)]
    total = ordered[0, 0:N, :].astype(f32)
    for y in range(1, Y):
        total = total * jnp.exp(logs[y]) + ordered[y, 0:N, :].astype(f32)
    rows = three_rows(jnp.broadcast_to(logs[0] + logs[1] + logs[2] + logs[3], (16, QUARTER)))
    total = total.astype(bf16)
    for z in range(Z):
        send[z, 0:SLICE, :] = total[z * SLICE : (z + 1) * SLICE]
        send[z, SLICE:, :] = rows


def prefix_kernel(got, back):
    state = jnp.zeros((SLICE, QUARTER), f32)
    for z in range(Z):
        back[z] = state.astype(bf16)
        decay = jnp.exp(log_row(got[z, SLICE : SLICE + 16, :]))
        state = state * decay + got[z, 0:SLICE, :].astype(f32)


def chip_kernel(at, before, part_0, part_1, part_2, part_3, send_0, send_1, send_2, send_3, ordered, states):
    in_order(at, (part_0, part_1, part_2, part_3), ordered)
    state = before[...].reshape(N, QUARTER).astype(f32)
    for y in range(Y):
        states[y] = state.astype(bf16)
        if y < Y - 1:
            decay = jnp.exp(log_row(ordered[y, N : N + 16, :]))
            state = state * decay + ordered[y, 0:N, :].astype(f32)
    for k, send in enumerate((send_0, send_1, send_2, send_3)):
        send[...] = states[lax.rem(at[1] + k, Y)]


def carried_kernel(at, within, queries, growth, state_0, state_1, state_2, state_3, scanned):
    for k, state in enumerate((state_0, state_1, state_2, state_3)):
        c0 = pl.multiple_of(lax.rem(at[1] + (Y - k), Y) * QUARTER, 128)
        columns = pl.ds(c0, QUARTER)
        carried = dot(queries[...], state[...]) * dot(growth[...], head_table(c0, QUARTER))
        scanned[:, columns] = (within[:, columns] + carried).astype(bf16)


def norm_kernel(at, scanned, scanned_other, gate, gate_other, gain, normed, whole, gates):
    core = at[0]
    own_at = pl.multiple_of(core * HALF, 128)
    other_at = pl.multiple_of((1 - core) * HALF, 128)
    whole[:, pl.ds(own_at, HALF)] = scanned[...]
    whole[:, pl.ds(other_at, HALF)] = scanned_other[...]
    gates[pl.ds(pl.multiple_of(core * ROWS, 128), ROWS), :] = gate[:, 0:GCH]
    gates[pl.ds(pl.multiple_of((1 - core) * ROWS, 128), ROWS), :] = gate_other[:, 0:GCH]

    def body(i, carry):
        rows = pl.ds(pl.multiple_of(i * 16, 16), 16)
        g = gates[rows, :].astype(f32)
        gated = whole[rows, :].astype(f32) * (g * jax.nn.sigmoid(g))
        scale = lax.rsqrt(jnp.mean(gated * gated, axis=1, keepdims=True) + 1e-05)
        normed[rows, :] = (gated * scale * gain[...]).astype(bf16)
        return carry

    lax.fori_loop(0, PAIR // 16, body, 0)


def project_kernel(at, normed, weight, *outs):
    total = dot(normed[...], weight[...])
    for i, out in enumerate(outs):

        @pl.when(pl.program_id(0) == i)
        def _(out=out):
            out[...] = total.astype(out.dtype)


def project(blocks, normed, weight, dtype):
    count = blocks.shape[0]

    def all_of(i, at):
        return (0, 0)

    return pl.pallas_call(
        project_kernel,
        out_shape=(shape(PAIR, BLOCK, dtype=dtype),) * count,
        grid_spec=pltpu.PrefetchScalarGridSpec(
            num_scalar_prefetch=1,
            grid=(count,),
            in_specs=[
                pl.BlockSpec((PAIR, GCH), all_of),
                pl.BlockSpec((GCH, BLOCK), lambda i, at: (0, at[i])),
            ],
            out_specs=[pl.BlockSpec((PAIR, BLOCK), all_of)] * count,
        ),
        cost_estimate=pl.CostEstimate(
            flops=2 * PAIR * GCH * BLOCK * count,
            bytes_accessed=2 * GCH * BLOCK * count,
            transcendentals=0,
        ),
        compiler_params=params(52),
        name="project",
    )(blocks, normed, weight)


def add_kernel(at, own, a, b, c, keep, away):
    core = at[0]
    for ref, which in ((keep, core), (away, 1 - core)):
        rows = pl.ds(pl.multiple_of(which * ROWS, 128), ROWS)
        total = own[rows, :] + a[rows, :].astype(f32) + b[rows, :].astype(f32)
        ref[...] = (total + c[rows, :].astype(f32)).astype(bf16)


def join_kernel(at, keep, got, out):
    core = at[0]
    out[:, pl.ds(pl.multiple_of(core * BLOCK, 128), BLOCK)] = keep[...]
    out[:, pl.ds(pl.multiple_of((1 - core) * BLOCK, 128), BLOCK)] = got[...]


def shape(*dims, dtype=bf16):
    return jax.ShapeDtypeStruct(dims, dtype)


def on_device(projected, conv_weight, conv_bias, step_bias, log_rates, norm_gain, out_weight):
    core, y, z, tp = (lax.axis_index(name) for name in ("c", "y", "z", "tp"))
    at = jnp.stack([core, y, z, tp]).astype(jnp.int32)
    weight = lax.all_gather(out_weight[0], ("z", "y", "c"), axis=0, tiled=True)
    mine = projected.reshape(ROWS, GCOLS)
    swap = [(0, 1), (1, 0)]
    other = lax.ppermute(mine, "c", swap)
    tail = mine[ROWS - 8 :, GCH : GCH + GCONV]
    all_axes = ("z", "y", "c")
    rim_0 = lax.ppermute(tail, all_axes, [(2 * i + 1, 2 * i + 2) for i in range(CHIPS - 1)])
    rim_1 = lax.ppermute(tail, all_axes, [(2 * i + 1, 2 * i + 3) for i in range(CHIPS - 1)])
    rim = jnp.where(core == 0, rim_0, rim_1)

    within, queries, growth, *sends = pl.pallas_call(
        scan_kernel,
        out_shape=(
            shape(PAIR, HALF, dtype=f32), shape(PAIR, N), shape(PAIR, 128),
        ) + (shape(N + 16, QUARTER),) * Y,
        in_specs=[smem()] + [vmem()] * 7,
        out_specs=(vmem(),) * (3 + Y),
        scratch_shapes=[
            pltpu.VMEM((PAIR + 8, HALF + 2 * N), f32),
            pltpu.VMEM((8, HALF + 2 * N), f32),
            pltpu.VMEM((PAIR, HALF), bf16),
            pltpu.VMEM((PAIR, N), bf16),
            pltpu.VMEM((PAIR, 128), f32),
            pltpu.VMEM((8, 128), f32),
        ],
        cost_estimate=pl.CostEstimate(
            flops=1 << 29, bytes_accessed=5 * MIB, transcendentals=1 << 20
        ),
        compiler_params=params(20),
        name="scan",
    )(at, mine, other, rim, conv_weight[0], conv_bias, step_bias, log_rates)

    def along_y(parts):
        moves = [[(i, (i + k) % Y) for i in range(Y)] for k in range(Y)]
        return [parts[0]] + [lax.ppermute(parts[k], "y", moves[k]) for k in range(1, Y)]

    parts = along_y(sends)
    plane = pl.pallas_call(
        plane_kernel,
        out_shape=shape(Z, SLICE + 16, QUARTER),
        in_specs=[smem()] + [vmem()] * Y,
        out_specs=vmem(),
        scratch_shapes=[pltpu.VMEM((Y, N + 16, QUARTER), bf16)],
        compiler_params=params(8),
        name="plane",
    )(at, *parts)
    plane = lax.all_to_all(plane, "z", 0, 0, tiled=True)
    back = pl.pallas_call(
        prefix_kernel,
        out_shape=shape(Z, SLICE, QUARTER),
        in_specs=[vmem()],
        out_specs=vmem(),
        compiler_params=params(8),
        name="prefix",
    )(plane)
    before = lax.all_to_all(back, "z", 0, 0, tiled=True)
    states = pl.pallas_call(
        chip_kernel,
        out_shape=(shape(N, QUARTER),) * Y,
        in_specs=[smem()] + [vmem()] * (1 + Y),
        out_specs=(vmem(),) * Y,
        scratch_shapes=[
            pltpu.VMEM((Y, N + 16, QUARTER), bf16),
            pltpu.VMEM((Y, N, QUARTER), bf16),
        ],
        compiler_params=params(8),
        name="chip",
    )(at, before, *parts)
    states = along_y(states)
    scanned = pl.pallas_call(
        carried_kernel,
        out_shape=shape(PAIR, HALF),
        in_specs=[smem()] + [vmem()] * (3 + Y),
        out_specs=vmem(),
        cost_estimate=pl.CostEstimate(flops=1 << 28, bytes_accessed=2 * MIB, transcendentals=0),
        compiler_params=params(8),
        name="carried",
    )(at, within, queries, growth, *states)

    normed = pl.pallas_call(
        norm_kernel,
        out_shape=shape(PAIR, GCH),
        in_specs=[smem()] + [vmem()] * 5,
        out_specs=vmem(),
        scratch_shapes=[pltpu.VMEM((PAIR, GCH), bf16), pltpu.VMEM((PAIR, GCH), bf16)],
        cost_estimate=pl.CostEstimate(
            flops=1 << 23, bytes_accessed=4 * MIB, transcendentals=1 << 19
        ),
        compiler_params=params(10),
        name="norm",
    )(at, scanned, lax.ppermute(scanned, "c", swap), mine, other, norm_gain)

    offsets = (2, 1, 3)
    places = lax.rem(tp + jnp.asarray(offsets + (0,), jnp.int32), T).astype(jnp.int32)
    blocks = places * C + core.astype(jnp.int32)
    shares = [
        lax.ppermute(part, "tp", [(i, (i + k) % T) for i in range(T)])
        for k, part in zip(offsets, project(blocks[:3], normed, weight, bf16), strict=True)
    ]
    (own_share,) = project(blocks[3:], normed, weight, f32)
    keep, away = pl.pallas_call(
        add_kernel,
        out_shape=(shape(ROWS, BLOCK), shape(ROWS, BLOCK)),
        in_specs=[smem()] + [vmem()] * 4,
        out_specs=(vmem(), vmem()),
        compiler_params=params(8),
        name="add",
    )(at, own_share, *shares)
    return pl.pallas_call(
        join_kernel,
        out_shape=shape(ROWS, C * BLOCK),
        in_specs=[smem(), vmem(), vmem()],
        out_specs=vmem(),
        compiler_params=params(8),
        name="join",
    )(at, keep, lax.ppermute(away, "c", swap))


def solution(mesh):
    chips = Mesh(mesh.devices.reshape(Z, Y, C, T), ("z", "y", "c", "tp"))
    ctx = ("z", "y", "c")
    return jax.shard_map(
        on_device,
        mesh=chips,
        in_specs=(
            P(ctx, "tp", None),
            P("tp", None, None),
            P("tp", None),
            P("tp", None),
            P("tp", None),
            P("tp", None),
            P("tp", ctx, None),
        ),
        out_specs=P(ctx, "tp"),
        check_vma=False,
    )
```

```python
import functools

import jax
import jax.numpy as jnp
from jax import lax
from jax.experimental import pallas as pl
from jax.experimental.pallas import tpu as pltpu
from jax.sharding import Mesh
from jax.sharding import PartitionSpec as P

P_SIZE = 64
N = 256
KCONV = 4
ROWS = 128
PAIR = 256
GCH = 2048
GCONV = 2560
GCOLS = 4640
HALF = 1024
HEADS = 16
QUARTER = HALF // 4
SLICE = N // 8
COLUMNS = 1024
WIDE = 512
Z, Y, C, T = 8, 4, 2, 4
CHIPS = Z * Y
f32, bf16 = jnp.float32, jnp.bfloat16
MIB = 1 << 20


def params(mib):
    return pltpu.CompilerParams(vmem_limit_bytes=mib * MIB)


def vmem():
    return pl.BlockSpec(memory_space=pltpu.VMEM)


def smem():
    return pl.BlockSpec(memory_space=pltpu.SMEM)


def dot(a, b, ca=1, cb=0, precision=None):
    return lax.dot_general(
        a, b, (((ca,), (cb,)), ((), ())), precision=precision, preferred_element_type=f32
    )


def lanes(shape):
    return lax.broadcasted_iota(jnp.int32, shape, 1)


def split_three(v):
    v = jnp.where(lanes(v.shape) < HEADS, v, 0.0)
    high = v.astype(bf16).astype(f32)
    rest = v - high
    middle = rest.astype(bf16).astype(f32)
    low = (rest - middle).astype(bf16).astype(f32)
    packed = high + pltpu.roll(middle, HEADS, 1) + pltpu.roll(low, 2 * HEADS, 1)
    return packed.astype(bf16)


def head_table(first, width):
    row = lax.broadcasted_iota(jnp.int32, (128, width), 0)
    column = lax.broadcasted_iota(jnp.int32, (128, width), 1) + first
    hit = (row < 3 * HEADS) & ((row % HEADS) == column // P_SIZE)
    return jnp.where(hit, 1.0, 0.0).astype(bf16)


def three_rows(v):
    row = lax.broadcasted_iota(jnp.int32, v.shape, 0)
    high = v.astype(bf16).astype(f32)
    middle = (v - high).astype(bf16).astype(f32)
    low = (v - high - middle).astype(bf16).astype(f32)
    picked = jnp.where(row == 0, high, jnp.where(row == 1, middle, jnp.where(row == 2, low, 0.0)))
    return picked.astype(bf16)


def log_row(rows):
    return jnp.sum(rows.astype(f32), axis=0, keepdims=True)


def scan_kernel(
    at, mine, other, rim, taps, bias, step_bias, log_rates,
    within, keys, growth, send_0, send_1, send_2, send_3,
    padded, tap_rows, values, queries, raw, small,
):
    core = at[0]
    x_at = pl.multiple_of(core * HALF, 128)
    mine_at = pl.multiple_of(core * ROWS, 128)
    other_at = pl.multiple_of((1 - core) * ROWS, 128)
    padded[0:8, 0:HALF] = rim[:, pl.ds(x_at, HALF)].astype(f32)
    padded[0:8, HALF:] = rim[:, GCH:GCONV].astype(f32)
    z_end = pl.multiple_of(GCH + x_at, 128)
    for rows, ref in ((mine_at, mine), (other_at, other)):
        target = pl.ds(pl.multiple_of(8 + rows, 8), ROWS)
        padded[target, 0:HALF] = ref[:, pl.ds(z_end, HALF)].astype(f32)
        padded[target, HALF:] = ref[:, 2 * GCH : GCH + GCONV].astype(f32)
        raw[pl.ds(rows, ROWS), :] = jnp.zeros((ROWS, 128), f32)
        raw[pl.ds(rows, ROWS), 0:32] = ref[:, GCH + GCONV : GCOLS].astype(f32)
    tap_rows[0:KCONV, 0:HALF] = taps[:, pl.ds(x_at, HALF)]
    tap_rows[0:KCONV, HALF:] = taps[:, GCH:GCONV]
    tap_rows[4:5, 0:HALF] = bias[:, pl.ds(x_at, HALF)]
    tap_rows[4:5, HALF:] = bias[:, GCH:GCONV]
    small[...] = jnp.zeros((8, 128), f32)
    small[0:1, 0:32] = step_bias[...]
    small[1:2, 0:32] = log_rates[...]

    for c0 in range(0, HALF + 2 * N, 256):
        for r0 in range(0, PAIR, 64):
            total = jnp.broadcast_to(tap_rows[4:5, c0 : c0 + 256], (64, 256))
            for k in range(KCONV):
                total = total + tap_rows[k : k + 1, c0 : c0 + 256] * padded[
                    5 + k + r0 : 5 + k + r0 + 64, c0 : c0 + 256
                ]
            active = (total * jax.nn.sigmoid(total)).astype(bf16)
            if c0 < HALF:
                values[r0 : r0 + 64, c0 : c0 + 256] = active
            elif c0 == HALF:
                keys[r0 : r0 + 64, :] = active
            else:
                queries[r0 : r0 + 64, :] = active

    first = core == 0

    def own(v):
        return jnp.where(first, v, pltpu.roll(v, 128 - HEADS, 1))

    head_lane = lanes((PAIR, 128)) < HEADS
    steps = own(raw[...] + small[0:1, :])
    steps = jnp.where(head_lane, jax.nn.softplus(steps), 0.0)
    rate = -jnp.exp(own(jnp.broadcast_to(small[1:2, :], (8, 128))))[0:1]
    logs = steps * rate
    row = lax.broadcasted_iota(jnp.int32, (PAIR, PAIR), 0)
    column = lax.broadcasted_iota(jnp.int32, (PAIR, PAIR), 1)
    running = dot(jnp.where(row >= column, 1.0, 0.0), logs, precision=lax.Precision.HIGHEST)
    running_t = running.T
    steps_t = steps.T
    growth[...] = split_three(jnp.exp(running))

    causal = row[:ROWS, :ROWS] >= column[:ROWS, :ROWS]
    products = []
    for a in (0, ROWS):
        own_product = dot(queries[a : a + ROWS, :], keys[a : a + ROWS, :], 1, 1)
        products.append(jnp.where(causal, own_product, 0.0))
    across = dot(queries[ROWS:, :], keys[:ROWS, :], 1, 1).astype(bf16)
    low_lane = lanes((ROWS, 128)) < P_SIZE
    for pair in range(HEADS // 2):
        c0 = pair * 128
        for i, a in enumerate((0, ROWS)):
            x = values[a : a + ROWS, c0 : c0 + 128]
            parts = []
            for h in (2 * pair, 2 * pair + 1):
                gap = running[a : a + ROWS, h : h + 1] - running_t[h : h + 1, a : a + ROWS]
                factor = products[i] * jnp.exp(jnp.minimum(gap, 0.0)) * steps_t[h : h + 1, a : a + ROWS]
                parts.append(dot(factor.astype(bf16), x))
            within[a : a + ROWS, c0 : c0 + 128] = jnp.where(low_lane, parts[0], parts[1])

    middle = running[ROWS - 1 : ROWS, :]
    end = running[PAIR - 1 : PAIR, :]
    to_end = split_three(jnp.exp(end - running) * steps)
    to_middle = split_three(jnp.exp(middle - running[:ROWS]) * steps[:ROWS])
    from_middle = split_three(jnp.exp(running[ROWS:] - middle))
    all_logs = split_three(jnp.broadcast_to(end, (16, 128)))
    keys_t = keys[...].astype(f32).T.astype(bf16)
    for k, send in enumerate((send_0, send_1, send_2, send_3)):
        c0 = pl.multiple_of(lax.rem(at[1] + k, Y) * QUARTER, 128)
        columns = pl.ds(c0, QUARTER)
        table = head_table(c0, QUARTER)
        x = values[:, columns].astype(f32)
        entering = dot(across, (x[:ROWS] * dot(to_middle, table)).astype(bf16))
        within[ROWS:, columns] += entering * dot(from_middle, table)
        weighted = (x * dot(to_end, table)).astype(bf16)
        send[0:N, :] = dot(keys_t, weighted).astype(bf16)
        send[N:, :] = three_rows(dot(all_logs, table))
    keys[...] = queries[...]


def in_order(at, parts, ordered):
    for k, part in enumerate(parts):
        ordered[lax.rem(at[1] + (Y - k), Y)] = part[...]


def plane_kernel(at, part_0, part_1, part_2, part_3, send, ordered):
    in_order(at, (part_0, part_1, part_2, part_3), ordered)
    logs = [log_row(ordered[y, N : N + 16, :]) for y in range(Y)]
    total = ordered[0, 0:N, :].astype(f32)
    for y in range(1, Y):
        total = total * jnp.exp(logs[y]) + ordered[y, 0:N, :].astype(f32)
    rows = three_rows(jnp.broadcast_to(logs[0] + logs[1] + logs[2] + logs[3], (16, QUARTER)))
    total = total.astype(bf16)
    for z in range(Z):
        send[z, 0:SLICE, :] = total[z * SLICE : (z + 1) * SLICE]
        send[z, SLICE:, :] = rows


def prefix_kernel(got, back):
    state = jnp.zeros((SLICE, QUARTER), f32)
    for z in range(Z):
        back[z] = state.astype(bf16)
        decay = jnp.exp(log_row(got[z, SLICE : SLICE + 16, :]))
        state = state * decay + got[z, 0:SLICE, :].astype(f32)


def chip_kernel(at, before, part_0, part_1, part_2, part_3, send_0, send_1, send_2, send_3, ordered, states):
    in_order(at, (part_0, part_1, part_2, part_3), ordered)
    state = before[...].reshape(N, QUARTER).astype(f32)
    for y in range(Y):
        states[y] = state.astype(bf16)
        if y < Y - 1:
            decay = jnp.exp(log_row(ordered[y, N : N + 16, :]))
            state = state * decay + ordered[y, 0:N, :].astype(f32)
    for k, send in enumerate((send_0, send_1, send_2, send_3)):
        send[...] = states[lax.rem(at[1] + k, Y)]


def carried_kernel(at, within, queries, growth, state_0, state_1, state_2, state_3, scanned):
    for k, state in enumerate((state_0, state_1, state_2, state_3)):
        c0 = pl.multiple_of(lax.rem(at[1] + (Y - k), Y) * QUARTER, 128)
        columns = pl.ds(c0, QUARTER)
        carried = dot(queries[...], state[...]) * dot(growth[...], head_table(c0, QUARTER))
        scanned[:, columns] = (within[:, columns] + carried).astype(bf16)


def split_kernel(at, scanned, keep, away):
    for ref, which in ((keep, at[0]), (away, 1 - at[0])):
        ref[...] = scanned[pl.ds(pl.multiple_of(which * ROWS, 128), ROWS), :]


def norm_kernel(at, keep, got, gate, gain, normed, whole):
    core = at[0]
    whole[:, pl.ds(pl.multiple_of(core * HALF, 128), HALF)] = keep[...]
    whole[:, pl.ds(pl.multiple_of((1 - core) * HALF, 128), HALF)] = got[...]

    def body(i, carry):
        rows = pl.ds(pl.multiple_of(i * 16, 16), 16)
        g = gate[rows, 0:GCH].astype(f32)
        gated = whole[rows, :].astype(f32) * (g * jax.nn.sigmoid(g))
        scale = lax.rsqrt(jnp.mean(gated * gated, axis=1, keepdims=True) + 1e-05)
        normed[rows, :] = (gated * scale * gain[...]).astype(bf16)
        return carry

    lax.fori_loop(0, ROWS // 16, body, 0)


def pick_kernel(at, weight, *parts):
    for k, part in enumerate(parts):
        first = pl.multiple_of(lax.rem(at[3] + k, T) * COLUMNS, 128)
        part[...] = weight[:, pl.ds(first, COLUMNS)]


def order_kernel(at, *refs):
    out = refs[-1]
    for k, part in enumerate(refs[:-1]):
        out[lax.rem(at[3] + (T - k), T)] = part[...]


def groups_kernel(at, own, behind, far_low, far_high, ahead, out):
    out[at[3]] = own[...]
    out[lax.rem(at[3] + 3, T)] = behind[...]
    out[lax.rem(at[3] + 1, T)] = ahead[...]
    far = lax.rem(at[3] + 2, T)
    out[far, 0 : ROWS // 2, :] = far_low[...]
    out[far, ROWS // 2 :, :] = far_high[...]


def project_kernel(normed, weight, out, total):
    group = pl.program_id(1)
    product = dot(normed[group], weight[...].reshape(GCH, weight.shape[-1]))

    @pl.when(group == 0)
    def _():
        total[...] = product

    @pl.when((group > 0) & (group < T - 1))
    def _():
        total[...] += product

    @pl.when(group == T - 1)
    def _():
        out[...] = (total[...] + product).astype(bf16)


def shape(*dims, dtype=bf16):
    return jax.ShapeDtypeStruct(dims, dtype)


def on_device(projected, conv_weight, conv_bias, step_bias, log_rates, norm_gain, out_weight):
    core, y, z, tp = (lax.axis_index(name) for name in ("c", "y", "z", "tp"))
    at = jnp.stack([core, y, z, tp]).astype(jnp.int32)
    parts = pl.pallas_call(
        pick_kernel,
        out_shape=(shape(32, COLUMNS),) * T,
        in_specs=[smem(), vmem()],
        out_specs=(vmem(),) * T,
        compiler_params=params(8),
        name="pick",
    )(at, out_weight[0])
    on = [[(i, (i + k) % T) for i in range(T)] for k in range(T)]
    rows = pl.pallas_call(
        order_kernel,
        out_shape=shape(T, 32, COLUMNS),
        in_specs=[smem()] + [vmem()] * T,
        out_specs=vmem(),
        compiler_params=params(8),
        name="order",
    )(at, parts[0], *[lax.ppermute(parts[k], "tp", on[k]) for k in (1, 2, 3)])
    weight = lax.all_gather(rows, ("z", "y", "c"), axis=0, tiled=True)
    weight = weight.reshape(CHIPS * C, T, 32, COLUMNS)
    mine = projected.reshape(ROWS, GCOLS)
    swap = [(0, 1), (1, 0)]
    other = lax.ppermute(mine, "c", swap)
    tail = mine[ROWS - 8 :, GCH : GCH + GCONV]
    all_axes = ("z", "y", "c")
    rim_0 = lax.ppermute(tail, all_axes, [(2 * i + 1, 2 * i + 2) for i in range(CHIPS - 1)])
    rim_1 = lax.ppermute(tail, all_axes, [(2 * i + 1, 2 * i + 3) for i in range(CHIPS - 1)])
    rim = jnp.where(core == 0, rim_0, rim_1)

    within, queries, growth, *sends = pl.pallas_call(
        scan_kernel,
        out_shape=(
            shape(PAIR, HALF, dtype=f32), shape(PAIR, N), shape(PAIR, 128),
        ) + (shape(N + 16, QUARTER),) * Y,
        in_specs=[smem()] + [vmem()] * 7,
        out_specs=(vmem(),) * (3 + Y),
        scratch_shapes=[
            pltpu.VMEM((PAIR + 8, HALF + 2 * N), f32),
            pltpu.VMEM((8, HALF + 2 * N), f32),
            pltpu.VMEM((PAIR, HALF), bf16),
            pltpu.VMEM((PAIR, N), bf16),
            pltpu.VMEM((PAIR, 128), f32),
            pltpu.VMEM((8, 128), f32),
        ],
        cost_estimate=pl.CostEstimate(
            flops=1 << 29, bytes_accessed=5 * MIB, transcendentals=1 << 20
        ),
        compiler_params=params(20),
        name="scan",
    )(at, mine, other, rim, conv_weight[0], conv_bias, step_bias, log_rates)

    def along_y(parts):
        moves = [[(i, (i + k) % Y) for i in range(Y)] for k in range(Y)]
        return [parts[0]] + [lax.ppermute(parts[k], "y", moves[k]) for k in range(1, Y)]

    parts = along_y(sends)
    plane = pl.pallas_call(
        plane_kernel,
        out_shape=shape(Z, SLICE + 16, QUARTER),
        in_specs=[smem()] + [vmem()] * Y,
        out_specs=vmem(),
        scratch_shapes=[pltpu.VMEM((Y, N + 16, QUARTER), bf16)],
        compiler_params=params(8),
        name="plane",
    )(at, *parts)
    plane = lax.all_to_all(plane, "z", 0, 0, tiled=True)
    back = pl.pallas_call(
        prefix_kernel,
        out_shape=shape(Z, SLICE, QUARTER),
        in_specs=[vmem()],
        out_specs=vmem(),
        compiler_params=params(8),
        name="prefix",
    )(plane)
    before = lax.all_to_all(back, "z", 0, 0, tiled=True)
    states = pl.pallas_call(
        chip_kernel,
        out_shape=(shape(N, QUARTER),) * Y,
        in_specs=[smem()] + [vmem()] * (1 + Y),
        out_specs=(vmem(),) * Y,
        scratch_shapes=[
            pltpu.VMEM((Y, N + 16, QUARTER), bf16),
            pltpu.VMEM((Y, N, QUARTER), bf16),
        ],
        compiler_params=params(8),
        name="chip",
    )(at, before, *parts)
    states = along_y(states)
    scanned = pl.pallas_call(
        carried_kernel,
        out_shape=shape(PAIR, HALF),
        in_specs=[smem()] + [vmem()] * (3 + Y),
        out_specs=vmem(),
        cost_estimate=pl.CostEstimate(flops=1 << 28, bytes_accessed=2 * MIB, transcendentals=0),
        compiler_params=params(8),
        name="carried",
    )(at, within, queries, growth, *states)

    keep, away = pl.pallas_call(
        split_kernel,
        out_shape=(shape(ROWS, HALF),) * 2,
        in_specs=[smem(), vmem()],
        out_specs=(vmem(),) * 2,
        compiler_params=params(8),
        name="split",
    )(at, scanned)
    normed = pl.pallas_call(
        norm_kernel,
        out_shape=shape(ROWS, GCH),
        in_specs=[smem()] + [vmem()] * 4,
        out_specs=vmem(),
        scratch_shapes=[pltpu.VMEM((ROWS, GCH), bf16)],
        cost_estimate=pl.CostEstimate(
            flops=1 << 22, bytes_accessed=2 * MIB, transcendentals=1 << 18
        ),
        compiler_params=params(10),
        name="norm",
    )(at, keep, lax.ppermute(away, "c", swap), mine, norm_gain)

    behind = lax.ppermute(normed, "tp", on[1])
    ahead = lax.ppermute(normed, "tp", on[3])
    far_low = lax.ppermute(behind[: ROWS // 2], "tp", on[1])
    far_high = lax.ppermute(ahead[ROWS // 2 :], "tp", on[3])
    groups = pl.pallas_call(
        groups_kernel,
        out_shape=shape(T, ROWS, GCH),
        in_specs=[smem()] + [vmem()] * 5,
        out_specs=vmem(),
        compiler_params=params(10),
        name="groups",
    )(at, normed, behind, far_low, far_high, ahead)
    return pl.pallas_call(
        project_kernel,
        grid=(COLUMNS // WIDE, T),
        out_shape=shape(ROWS, COLUMNS),
        in_specs=[
            vmem(),
            pl.BlockSpec((CHIPS * C, 1, 32, WIDE), lambda n, g: (0, g, 0, n)),
        ],
        out_specs=pl.BlockSpec((ROWS, WIDE), lambda n, g: (0, n)),
        scratch_shapes=[pltpu.VMEM((ROWS, WIDE), f32)],
        cost_estimate=pl.CostEstimate(
            flops=2 * ROWS * T * GCH * COLUMNS,
            bytes_accessed=2 * T * GCH * COLUMNS,
            transcendentals=0,
        ),
        compiler_params=params(50),
        name="project",
    )(groups, weight)


def solution(mesh):
    chips = Mesh(mesh.devices.reshape(Z, Y, C, T), ("z", "y", "c", "tp"))
    ctx = ("z", "y", "c")
    return jax.shard_map(
        on_device,
        mesh=chips,
        in_specs=(
            P(ctx, "tp", None),
            P("tp", None, None),
            P("tp", None),
            P("tp", None),
            P("tp", None),
            P("tp", None),
            P("tp", ctx, None),
        ),
        out_specs=P(ctx, "tp"),
        check_vma=False,
    )
```

```python
import functools

import jax
import jax.numpy as jnp
from jax import lax
from jax.experimental import pallas as pl
from jax.experimental.pallas import tpu as pltpu
from jax.sharding import Mesh
from jax.sharding import PartitionSpec as P

P_SIZE = 64
N = 256
KCONV = 4
ROWS = 128
PAIR = 256
GCH = 2048
GCONV = 2560
GCOLS = 4640
HALF = 1024
HEADS = 16
QUARTER = HALF // 4
SLICE = N // 8
COLUMNS = 1024
WIDE = 512
Z, Y, C, T = 8, 4, 2, 4
CHIPS = Z * Y
f32, bf16 = jnp.float32, jnp.bfloat16
MIB = 1 << 20


def params(mib):
    return pltpu.CompilerParams(vmem_limit_bytes=mib * MIB)


def vmem():
    return pl.BlockSpec(memory_space=pltpu.VMEM)


def smem():
    return pl.BlockSpec(memory_space=pltpu.SMEM)


def dot(a, b, ca=1, cb=0, precision=None):
    return lax.dot_general(
        a, b, (((ca,), (cb,)), ((), ())), precision=precision, preferred_element_type=f32
    )


def lanes(shape):
    return lax.broadcasted_iota(jnp.int32, shape, 1)


def split_three(v):
    v = jnp.where(lanes(v.shape) < HEADS, v, 0.0)
    high = v.astype(bf16).astype(f32)
    rest = v - high
    middle = rest.astype(bf16).astype(f32)
    low = (rest - middle).astype(bf16).astype(f32)
    packed = high + pltpu.roll(middle, HEADS, 1) + pltpu.roll(low, 2 * HEADS, 1)
    return packed.astype(bf16)


def head_table(first, width):
    row = lax.broadcasted_iota(jnp.int32, (128, width), 0)
    column = lax.broadcasted_iota(jnp.int32, (128, width), 1) + first
    hit = (row < 3 * HEADS) & ((row % HEADS) == column // P_SIZE)
    return jnp.where(hit, 1.0, 0.0).astype(bf16)


def three_rows(v):
    row = lax.broadcasted_iota(jnp.int32, v.shape, 0)
    high = v.astype(bf16).astype(f32)
    middle = (v - high).astype(bf16).astype(f32)
    low = (v - high - middle).astype(bf16).astype(f32)
    picked = jnp.where(row == 0, high, jnp.where(row == 1, middle, jnp.where(row == 2, low, 0.0)))
    return picked.astype(bf16)


def log_row(rows):
    return jnp.sum(rows.astype(f32), axis=0, keepdims=True)


def scan_kernel(
    at, mine, other, rim, taps, bias, step_bias, log_rates,
    within, keys, growth, send_0, send_1, send_2, send_3,
    padded, tap_rows, values, queries, raw, small,
):
    core = at[0]
    x_at = pl.multiple_of(core * HALF, 128)
    mine_at = pl.multiple_of(core * ROWS, 128)
    other_at = pl.multiple_of((1 - core) * ROWS, 128)
    padded[0:8, 0:HALF] = rim[:, pl.ds(x_at, HALF)].astype(f32)
    padded[0:8, HALF:] = rim[:, GCH:GCONV].astype(f32)
    z_end = pl.multiple_of(GCH + x_at, 128)
    for rows, ref in ((mine_at, mine), (other_at, other)):
        target = pl.ds(pl.multiple_of(8 + rows, 8), ROWS)
        padded[target, 0:HALF] = ref[:, pl.ds(z_end, HALF)].astype(f32)
        padded[target, HALF:] = ref[:, 2 * GCH : GCH + GCONV].astype(f32)
        raw[pl.ds(rows, ROWS), :] = jnp.zeros((ROWS, 128), f32)
        raw[pl.ds(rows, ROWS), 0:32] = ref[:, GCH + GCONV : GCOLS].astype(f32)
    tap_rows[0:KCONV, 0:HALF] = taps[:, pl.ds(x_at, HALF)]
    tap_rows[0:KCONV, HALF:] = taps[:, GCH:GCONV]
    tap_rows[4:5, 0:HALF] = bias[:, pl.ds(x_at, HALF)]
    tap_rows[4:5, HALF:] = bias[:, GCH:GCONV]
    small[...] = jnp.zeros((8, 128), f32)
    small[0:1, 0:32] = step_bias[...]
    small[1:2, 0:32] = log_rates[...]

    for c0 in range(0, HALF + 2 * N, 256):
        for r0 in range(0, PAIR, 64):
            total = jnp.broadcast_to(tap_rows[4:5, c0 : c0 + 256], (64, 256))
            for k in range(KCONV):
                total = total + tap_rows[k : k + 1, c0 : c0 + 256] * padded[
                    5 + k + r0 : 5 + k + r0 + 64, c0 : c0 + 256
                ]
            active = (total * jax.nn.sigmoid(total)).astype(bf16)
            if c0 < HALF:
                values[r0 : r0 + 64, c0 : c0 + 256] = active
            elif c0 == HALF:
                keys[r0 : r0 + 64, :] = active
            else:
                queries[r0 : r0 + 64, :] = active

    first = core == 0

    def own(v):
        return jnp.where(first, v, pltpu.roll(v, 128 - HEADS, 1))

    head_lane = lanes((PAIR, 128)) < HEADS
    steps = own(raw[...] + small[0:1, :])
    steps = jnp.where(head_lane, jax.nn.softplus(steps), 0.0)
    rate = -jnp.exp(own(jnp.broadcast_to(small[1:2, :], (8, 128))))[0:1]
    logs = steps * rate
    row = lax.broadcasted_iota(jnp.int32, (PAIR, PAIR), 0)
    column = lax.broadcasted_iota(jnp.int32, (PAIR, PAIR), 1)
    running = dot(jnp.where(row >= column, 1.0, 0.0), logs, precision=lax.Precision.HIGHEST)
    running_t = running.T
    steps_t = steps.T
    growth[...] = split_three(jnp.exp(running))

    causal = row[:ROWS, :ROWS] >= column[:ROWS, :ROWS]
    products = []
    for a in (0, ROWS):
        own_product = dot(queries[a : a + ROWS, :], keys[a : a + ROWS, :], 1, 1)
        products.append(jnp.where(causal, own_product, 0.0))
    across = dot(queries[ROWS:, :], keys[:ROWS, :], 1, 1).astype(bf16)
    low_lane = lanes((ROWS, 128)) < P_SIZE
    for pair in range(HEADS // 2):
        c0 = pair * 128
        for i, a in enumerate((0, ROWS)):
            x = values[a : a + ROWS, c0 : c0 + 128]
            parts = []
            for h in (2 * pair, 2 * pair + 1):
                gap = running[a : a + ROWS, h : h + 1] - running_t[h : h + 1, a : a + ROWS]
                factor = products[i] * jnp.exp(jnp.minimum(gap, 0.0)) * steps_t[h : h + 1, a : a + ROWS]
                parts.append(dot(factor.astype(bf16), x))
            within[a : a + ROWS, c0 : c0 + 128] = jnp.where(low_lane, parts[0], parts[1])

    middle = running[ROWS - 1 : ROWS, :]
    end = running[PAIR - 1 : PAIR, :]
    to_end = split_three(jnp.exp(end - running) * steps)
    to_middle = split_three(jnp.exp(middle - running[:ROWS]) * steps[:ROWS])
    from_middle = split_three(jnp.exp(running[ROWS:] - middle))
    all_logs = split_three(jnp.broadcast_to(end, (16, 128)))
    keys_t = keys[...].astype(f32).T.astype(bf16)
    for k, send in enumerate((send_0, send_1, send_2, send_3)):
        c0 = pl.multiple_of(lax.rem(at[1] + k, Y) * QUARTER, 128)
        columns = pl.ds(c0, QUARTER)
        table = head_table(c0, QUARTER)
        x = values[:, columns].astype(f32)
        entering = dot(across, (x[:ROWS] * dot(to_middle, table)).astype(bf16))
        within[ROWS:, columns] += entering * dot(from_middle, table)
        weighted = (x * dot(to_end, table)).astype(bf16)
        send[0:N, :] = dot(keys_t, weighted).astype(bf16)
        send[N:, :] = three_rows(dot(all_logs, table))
    keys[...] = queries[...]


def in_order(at, parts, ordered):
    for k, part in enumerate(parts):
        ordered[lax.rem(at[1] + (Y - k), Y)] = part[...]


def plane_kernel(at, part_0, part_1, part_2, part_3, send, ordered):
    in_order(at, (part_0, part_1, part_2, part_3), ordered)
    logs = [log_row(ordered[y, N : N + 16, :]) for y in range(Y)]
    total = ordered[0, 0:N, :].astype(f32)
    for y in range(1, Y):
        total = total * jnp.exp(logs[y]) + ordered[y, 0:N, :].astype(f32)
    rows = three_rows(jnp.broadcast_to(logs[0] + logs[1] + logs[2] + logs[3], (16, QUARTER)))
    total = total.astype(bf16)
    for z in range(Z):
        send[z, 0:SLICE, :] = total[z * SLICE : (z + 1) * SLICE]
        send[z, SLICE:, :] = rows


def prefix_kernel(got, back):
    state = jnp.zeros((SLICE, QUARTER), f32)
    for z in range(Z):
        back[z] = state.astype(bf16)
        decay = jnp.exp(log_row(got[z, SLICE : SLICE + 16, :]))
        state = state * decay + got[z, 0:SLICE, :].astype(f32)


def chip_kernel(at, before, part_0, part_1, part_2, part_3, send_0, send_1, send_2, send_3, ordered, states):
    in_order(at, (part_0, part_1, part_2, part_3), ordered)
    state = before[...].reshape(N, QUARTER).astype(f32)
    for y in range(Y):
        states[y] = state.astype(bf16)
        if y < Y - 1:
            decay = jnp.exp(log_row(ordered[y, N : N + 16, :]))
            state = state * decay + ordered[y, 0:N, :].astype(f32)
    for k, send in enumerate((send_0, send_1, send_2, send_3)):
        send[...] = states[lax.rem(at[1] + k, Y)]


def carried_kernel(at, within, queries, growth, state_0, state_1, state_2, state_3, scanned):
    for k, state in enumerate((state_0, state_1, state_2, state_3)):
        c0 = pl.multiple_of(lax.rem(at[1] + (Y - k), Y) * QUARTER, 128)
        columns = pl.ds(c0, QUARTER)
        carried = dot(queries[...], state[...]) * dot(growth[...], head_table(c0, QUARTER))
        scanned[:, columns] = (within[:, columns] + carried).astype(bf16)


def split_kernel(at, scanned, keep, away):
    for ref, which in ((keep, at[0]), (away, 1 - at[0])):
        ref[...] = scanned[pl.ds(pl.multiple_of(which * ROWS, 128), ROWS), :]


def norm_kernel(at, keep, got, gate, gain, normed, whole):
    core = at[0]
    whole[:, pl.ds(pl.multiple_of(core * HALF, 128), HALF)] = keep[...]
    whole[:, pl.ds(pl.multiple_of((1 - core) * HALF, 128), HALF)] = got[...]

    def body(i, carry):
        rows = pl.ds(pl.multiple_of(i * 16, 16), 16)
        g = gate[rows, 0:GCH].astype(f32)
        gated = whole[rows, :].astype(f32) * (g * jax.nn.sigmoid(g))
        scale = lax.rsqrt(jnp.mean(gated * gated, axis=1, keepdims=True) + 1e-05)
        normed[rows, :] = (gated * scale * gain[...]).astype(bf16)
        return carry

    lax.fori_loop(0, ROWS // 16, body, 0)


def pick_kernel(at, weight, *parts):
    for k, part in enumerate(parts):
        first = pl.multiple_of(lax.rem(at[3] + k, T) * COLUMNS, 128)
        part[...] = weight[:, pl.ds(first, COLUMNS)]


def order_kernel(at, *refs):
    out = refs[-1]
    for k, part in enumerate(refs[:-1]):
        out[lax.rem(at[3] + (T - k), T)] = part[...]


def groups_kernel(at, own, behind, far_low, far_high, ahead, out):
    out[at[3]] = own[...]
    out[lax.rem(at[3] + 3, T)] = behind[...]
    out[lax.rem(at[3] + 1, T)] = ahead[...]
    far = lax.rem(at[3] + 2, T)
    out[far, 0 : ROWS // 2, :] = far_low[...]
    out[far, ROWS // 2 :, :] = far_high[...]


def project_kernel(normed, lower, upper, out, total):
    group = pl.program_id(1)
    product = dot(normed[group, :, 0:HALF], lower[...].reshape(HALF, WIDE))
    product = product + dot(normed[group, :, HALF:], upper[...].reshape(HALF, WIDE))

    @pl.when(group == 0)
    def _():
        total[...] = product

    @pl.when((group > 0) & (group < T - 1))
    def _():
        total[...] += product

    @pl.when(group == T - 1)
    def _():
        out[...] = (total[...] + product).astype(bf16)


def shape(*dims, dtype=bf16):
    return jax.ShapeDtypeStruct(dims, dtype)


def on_device(projected, conv_weight, conv_bias, step_bias, log_rates, norm_gain, out_weight):
    core, y, z, tp = (lax.axis_index(name) for name in ("c", "y", "z", "tp"))
    at = jnp.stack([core, y, z, tp]).astype(jnp.int32)
    parts = pl.pallas_call(
        pick_kernel,
        grid=(1,),
        out_shape=(shape(32, COLUMNS),) * T,
        in_specs=[smem(), pl.BlockSpec((32, T * COLUMNS), lambda i: (0, 0))],
        out_specs=(pl.BlockSpec((32, COLUMNS), lambda i: (0, 0)),) * T,
        compiler_params=params(8),
        name="pick",
    )(at, out_weight[0])
    on = [[(i, (i + k) % T) for i in range(T)] for k in range(T)]
    rows = pl.pallas_call(
        order_kernel,
        out_shape=shape(T, 32, COLUMNS),
        in_specs=[smem()] + [vmem()] * T,
        out_specs=vmem(),
        compiler_params=params(8),
        name="order",
    )(at, parts[0], *[lax.ppermute(parts[k], "tp", on[k]) for k in (1, 2, 3)])
    weight = lax.all_gather(rows, ("z", "y", "c"), axis=0, tiled=True)
    weight = weight.reshape(CHIPS * C, T, 32, COLUMNS)
    mine = projected.reshape(ROWS, GCOLS)
    swap = [(0, 1), (1, 0)]
    other = lax.ppermute(mine, "c", swap)
    tail = mine[ROWS - 8 :, GCH : GCH + GCONV]
    all_axes = ("z", "y", "c")
    rim_0 = lax.ppermute(tail, all_axes, [(2 * i + 1, 2 * i + 2) for i in range(CHIPS - 1)])
    rim_1 = lax.ppermute(tail, all_axes, [(2 * i + 1, 2 * i + 3) for i in range(CHIPS - 1)])
    rim = jnp.where(core == 0, rim_0, rim_1)

    within, queries, growth, *sends = pl.pallas_call(
        scan_kernel,
        out_shape=(
            shape(PAIR, HALF, dtype=f32), shape(PAIR, N), shape(PAIR, 128),
        ) + (shape(N + 16, QUARTER),) * Y,
        in_specs=[smem()] + [vmem()] * 7,
        out_specs=(vmem(),) * (3 + Y),
        scratch_shapes=[
            pltpu.VMEM((PAIR + 8, HALF + 2 * N), f32),
            pltpu.VMEM((8, HALF + 2 * N), f32),
            pltpu.VMEM((PAIR, HALF), bf16),
            pltpu.VMEM((PAIR, N), bf16),
            pltpu.VMEM((PAIR, 128), f32),
            pltpu.VMEM((8, 128), f32),
        ],
        cost_estimate=pl.CostEstimate(
            flops=1 << 29, bytes_accessed=5 * MIB, transcendentals=1 << 20
        ),
        compiler_params=params(20),
        name="scan",
    )(at, mine, other, rim, conv_weight[0], conv_bias, step_bias, log_rates)

    def along_y(parts):
        moves = [[(i, (i + k) % Y) for i in range(Y)] for k in range(Y)]
        return [parts[0]] + [lax.ppermute(parts[k], "y", moves[k]) for k in range(1, Y)]

    parts = along_y(sends)
    plane = pl.pallas_call(
        plane_kernel,
        out_shape=shape(Z, SLICE + 16, QUARTER),
        in_specs=[smem()] + [vmem()] * Y,
        out_specs=vmem(),
        scratch_shapes=[pltpu.VMEM((Y, N + 16, QUARTER), bf16)],
        compiler_params=params(8),
        name="plane",
    )(at, *parts)
    plane = lax.all_to_all(plane, "z", 0, 0, tiled=True)
    back = pl.pallas_call(
        prefix_kernel,
        out_shape=shape(Z, SLICE, QUARTER),
        in_specs=[vmem()],
        out_specs=vmem(),
        compiler_params=params(8),
        name="prefix",
    )(plane)
    before = lax.all_to_all(back, "z", 0, 0, tiled=True)
    states = pl.pallas_call(
        chip_kernel,
        out_shape=(shape(N, QUARTER),) * Y,
        in_specs=[smem()] + [vmem()] * (1 + Y),
        out_specs=(vmem(),) * Y,
        scratch_shapes=[
            pltpu.VMEM((Y, N + 16, QUARTER), bf16),
            pltpu.VMEM((Y, N, QUARTER), bf16),
        ],
        compiler_params=params(8),
        name="chip",
    )(at, before, *parts)
    states = along_y(states)
    scanned = pl.pallas_call(
        carried_kernel,
        out_shape=shape(PAIR, HALF),
        in_specs=[smem()] + [vmem()] * (3 + Y),
        out_specs=vmem(),
        cost_estimate=pl.CostEstimate(flops=1 << 28, bytes_accessed=2 * MIB, transcendentals=0),
        compiler_params=params(8),
        name="carried",
    )(at, within, queries, growth, *states)

    keep, away = pl.pallas_call(
        split_kernel,
        out_shape=(shape(ROWS, HALF),) * 2,
        in_specs=[smem(), vmem()],
        out_specs=(vmem(),) * 2,
        compiler_params=params(8),
        name="split",
    )(at, scanned)
    normed = pl.pallas_call(
        norm_kernel,
        out_shape=shape(ROWS, GCH),
        in_specs=[smem()] + [vmem()] * 4,
        out_specs=vmem(),
        scratch_shapes=[pltpu.VMEM((ROWS, GCH), bf16)],
        cost_estimate=pl.CostEstimate(
            flops=1 << 22, bytes_accessed=2 * MIB, transcendentals=1 << 18
        ),
        compiler_params=params(10),
        name="norm",
    )(at, keep, lax.ppermute(away, "c", swap), mine, norm_gain)

    behind = lax.ppermute(normed, "tp", on[1])
    ahead = lax.ppermute(normed, "tp", on[3])
    far_low = lax.ppermute(behind[: ROWS // 2], "tp", on[1])
    far_high = lax.ppermute(ahead[ROWS // 2 :], "tp", on[3])
    groups = pl.pallas_call(
        groups_kernel,
        out_shape=shape(T, ROWS, GCH),
        in_specs=[smem()] + [vmem()] * 5,
        out_specs=vmem(),
        compiler_params=params(10),
        name="groups",
    )(at, normed, behind, far_low, far_high, ahead)
    return pl.pallas_call(
        project_kernel,
        grid=(COLUMNS // WIDE, T),
        out_shape=shape(ROWS, COLUMNS),
        in_specs=[
            vmem(),
            pl.BlockSpec((CHIPS, 1, 32, WIDE), lambda n, g: (0, g, 0, n)),
            pl.BlockSpec((CHIPS, 1, 32, WIDE), lambda n, g: (1, g, 0, n)),
        ],
        out_specs=pl.BlockSpec((ROWS, WIDE), lambda n, g: (0, n)),
        scratch_shapes=[pltpu.VMEM((ROWS, WIDE), f32)],
        cost_estimate=pl.CostEstimate(
            flops=2 * ROWS * T * GCH * COLUMNS,
            bytes_accessed=2 * T * GCH * COLUMNS,
            transcendentals=0,
        ),
        compiler_params=params(50),
        name="project",
    )(groups, weight, weight)


def solution(mesh):
    chips = Mesh(mesh.devices.reshape(Z, Y, C, T), ("z", "y", "c", "tp"))
    ctx = ("z", "y", "c")
    return jax.shard_map(
        on_device,
        mesh=chips,
        in_specs=(
            P(ctx, "tp", None),
            P("tp", None, None),
            P("tp", None),
            P("tp", None),
            P("tp", None),
            P("tp", None),
            P("tp", ctx, None),
        ),
        out_specs=P(ctx, "tp"),
        check_vma=False,
    )
```
